256 devices in a mesh: seq: 128 (over x_lo, y, z, core), head: 2 (over x_hi).
Axes of the slice: x: 4 (x_hi: 2, x_lo: 2; x = x_hi * 2 + x_lo), y: 4, z: 8, core: 2. Of those that a mesh axis runs over, the one named last changes fastest.
Arguments:
- queries: bfloat16 [16384, 3072], P('seq', 'head'), may hold values from -6 to 6
- keys: bfloat16 [16384, 3072], P('seq', 'head'), may hold values from -6 to 6
- values: bfloat16 [16384, 3072], P('seq', 'head'), may hold values from -6 to 6
- cache_k: bfloat16 [2048, 3072], P('seq', 'head'), may hold values from -6 to 6
- cache_v: bfloat16 [2048, 3072], P('seq', 'head'), may hold values from -6 to 6
- sink_k: bfloat16 [8, 3072], P(None, 'head'), may hold values from -6 to 6
- sink_v: bfloat16 [8, 3072], P(None, 'head'), may hold values from -6 to 6
- suffix_lengths: int32 [32], replicated, may hold values from 1 to 1024, 16384 in all
- request_group: int32 [32], replicated, may hold values from 0 to 1
- w_out: bfloat16 [3072, 3072], P('head'), may hold values from -0.109375 to 0.109375
Outputs:
- projected: bfloat16 [3072, 16384], P('head', 'seq')
The draws below stay inside these ranges and needn't reach their ends.
All inputs are finite; a program needn't handle non-finite values.
Results may differ from the reference program's by a relative error of at most 0.011.
Values may be sent and summed in bfloat16 or wider, within the bound.
No kernel may reach another device: no remote copies, remote signals or barrier semaphores. Data moves between devices by JAX's collectives and lax.ppermute only.
A program may use at most 128 MiB of HBM per device.

```python
import math
import jax
import jax.numpy as jnp
import numpy as np
from jax import lax

D = 3072
HEADS = 32
HD = 96
W = 1024
SINKS = 4
G = 2
HC = 3072
SUF = 16384
REQS = 32


def draw_queries(key, part):
    field = jnp.clip(jax.random.normal(jax.random.fold_in(key, 11), (SUF, HC), jnp.float32), -6.0, 6.0)
    return field.astype(jnp.bfloat16)


def draw_keys(key, part):
    field = jnp.clip(jax.random.normal(jax.random.fold_in(key, 13), (SUF, HC), jnp.float32), -6.0, 6.0)
    return field.astype(jnp.bfloat16)


def place_ends(values, own_key, least, top_value):
    longest = values.shape.index(max(values.shape))
    spots = []
    for shift in (0, 1):
        where = [jax.random.randint(jax.random.fold_in(own_key, axis), (), 0, length) for axis, length in enumerate(values.shape)]
        where[longest] = (where[longest] + shift) % values.shape[longest]
        spots.append(tuple(where))
    return values.at[spots[0]].set(least).at[spots[1]].set(top_value)


def shard_levels(key, extent, cuts, low, largest):
    def one(dim, shards_of):
        heights = jax.random.uniform(jax.random.fold_in(jax.random.fold_in(key, 6), dim), (shards_of,), jnp.float32, low / len(cuts), largest / len(cuts))
        return jnp.repeat(jnp.exp(heights), extent[dim] // shards_of).reshape((-1,) + (1,) * (len(extent) - dim - 1))

    gain = one(*cuts[0])
    for cut in cuts[1:]:
        gain = gain * one(*cut)
    return gain


def length_profile(count, total, reach, lean):
    portions = [(1 << 20) // math.isqrt(standing ** lean) + 1 for standing in range(2, count + 1)]
    spare, holding = total - reach - (count - 1), [1] * (count - 1)
    while spare > 0:
        candidates = [i for i in range(count - 1) if holding[i] < reach]
        pool, left = sum([portions[i] for i in candidates]), spare
        for i in candidates:
            addition = min(reach - holding[i], max(1, left * portions[i] // pool), spare)
            holding[i] = holding[i] + addition
            spare = spare - addition
    return np.array([reach] + holding)


def uneven_parts(key, number_of, total, most, skew):
    if number_of == 2:
        one = jax.random.randint(key, (), max(1, total - most), min(most, total - 1) + 1)
        return jnp.stack([one, total - one])
    tallies = jnp.asarray(length_profile(number_of, total, most, skew), jnp.int32)
    pairs = (number_of - 1) // 2
    giver, taker = tallies[1:1 + 2 * pairs:2], tallies[2:2 + 2 * pairs:2]
    room = jnp.minimum(giver - 1, most - taker)
    passed = jax.random.randint(jax.random.fold_in(key, 1), (pairs,), 0, 1 << 20) % (room + 1)
    tallies = tallies.at[1:1 + 2 * pairs:2].set(giver - passed).at[2:2 + 2 * pairs:2].set(taker + passed)
    return tallies[jax.random.permutation(jax.random.fold_in(key, 2), number_of)]


def noise(key, dims, width, most, split=(), kind=jnp.bfloat16):
    result = jax.random.normal(key, dims, jnp.float32) * width
    if len(split) > 0:
        result = shard_levels(key, dims, split, -0.22, 0.18) * result
    return jnp.clip(result, min=-most, max=most).astype(kind)


def setup_inputs(seed: int = 0) -> dict:
    seeds = jax.random.split(jax.random.key(seed), 11)
    return {
        "queries": draw_queries(jax.random.fold_in(seeds[10], 71), 0),
        "keys": draw_keys(jax.random.fold_in(seeds[10], 71), 0),
        "values": noise(seeds[2], (SUF, HC), 1.0, 6.0, ((0, 128), (1, 2))),
        "cache_k": noise(seeds[3], (G * W, HC), 1.0, 6.0, ((0, 128), (1, 2))),
        "cache_v": noise(seeds[4], (G * W, HC), 1.0, 6.0, ((0, 128), (1, 2))),
        "sink_k": noise(seeds[5], (G * SINKS, HC), 1.0, 6.0, ((1, 2),)),
        "sink_v": noise(seeds[6], (G * SINKS, HC), 1.0, 6.0, ((1, 2),)),
        "suffix_lengths": uneven_parts(seeds[7], REQS, SUF, W, 2).astype(jnp.int32),
        "request_group": place_ends(jax.random.randint(seeds[8], (REQS,), 0, G), jax.random.fold_in(seeds[8], 1), 0, G - 1).astype(jnp.int32),
        "w_out": noise(seeds[9], (HC, D), HC ** -0.5, 0.109375, ((0, 2),)),
    }


def describe(index, starts, lengths, groups):
    inside = (starts[None, :] <= index[:, None]) & (index[:, None] < (starts + lengths)[None, :])
    flag = inside.astype(jnp.int32)
    found = lax.optimization_barrier(jnp.sum(flag, axis=1))
    request = lax.optimization_barrier(jnp.sum(flag * jnp.arange(starts.shape[0], dtype=jnp.int32)[None, :], axis=1))
    request = jnp.where(found > 0, request, -1).astype(jnp.int32)
    offset = (index - lax.optimization_barrier(jnp.sum(flag * starts[None, :], axis=1))).astype(jnp.int32)
    group = lax.optimization_barrier(jnp.sum(flag * groups[None, :], axis=1)).astype(jnp.int32)
    return (request, offset, group)

def reference(queries, keys, values, cache_k, cache_v, sink_k, sink_v, suffix_lengths, request_group, w_out):
    block = math.gcd(512, SUF)
    starts = (jnp.cumsum(suffix_lengths) - suffix_lengths).astype(jnp.int32)
    scale = 1.0 / math.sqrt(HD)
    zeros = jnp.zeros((W, HC), keys.dtype)
    keys_pad = jnp.concatenate([zeros, keys], axis=0)
    values_pad = jnp.concatenate([zeros, values], axis=0)
    sink_group = (jnp.arange(G * SINKS, dtype=jnp.int32) // SINKS).astype(jnp.int32)
    slot = jnp.arange(G * W, dtype=jnp.int32)

    def one_block(number):
        first = (number * block).astype(jnp.int32)
        index = first + jnp.arange(block, dtype=jnp.int32)
        req_q, off_q, grp_q = describe(index, starts, suffix_lengths, request_group)
        near = first - W + jnp.arange(W + block, dtype=jnp.int32)
        req_k, off_k, grp_k = describe(near, starts, suffix_lengths, request_group)
        mask_sink = grp_q[:, None] == sink_group[None, :]
        mask_cache = (grp_q[:, None] == (slot // W)[None, :]) & ((slot % W)[None, :] > off_q[:, None])
        mask_suf = (req_k[None, :] == req_q[:, None]) & (near[None, :] <= index[:, None]) & (index[:, None] - near[None, :] < W) & (near[None, :] >= 0)
        mask = jnp.concatenate([mask_sink, mask_cache, mask_suf], axis=1)
        near_k = lax.dynamic_slice_in_dim(keys_pad, first, W + block, 0)
        near_v = lax.dynamic_slice_in_dim(values_pad, first, W + block, 0)
        all_k = jnp.concatenate([sink_k, cache_k, near_k], axis=0).astype(jnp.float32).reshape(-1, HEADS, HD)
        all_v = jnp.concatenate([sink_v, cache_v, near_v], axis=0).astype(jnp.float32).reshape(-1, HEADS, HD)
        q_block = lax.dynamic_slice_in_dim(queries, first, block, 0).astype(jnp.float32).reshape(block, HEADS, HD)
        score = jnp.einsum('qhd,khd->hqk', q_block, all_k) * scale
        score = jnp.where(mask[None], score, jnp.float32(-1e+30))
        top = lax.optimization_barrier(jnp.max(score, axis=2, keepdims=True))
        prob = jnp.where(mask[None], jnp.exp(score - top), jnp.float32(0.0))
        den = lax.optimization_barrier(jnp.sum(prob, axis=2))
        weights = lax.optimization_barrier(prob.astype(jnp.bfloat16)).astype(jnp.float32)
        num = jnp.einsum('hqk,khd->hqd', weights, all_v)
        attn = (num / den[:, :, None]).transpose(1, 0, 2).reshape(block, HC)
        return attn.astype(jnp.bfloat16)
    attn = lax.map(one_block, jnp.arange(SUF // block, dtype=jnp.int32)).reshape(SUF, HC)
    out = jnp.dot(attn.astype(jnp.float32), w_out.astype(jnp.float32), preferred_element_type=jnp.float32)
    return out.T.astype(jnp.bfloat16)
```

```python
import functools
import math

import jax
import jax.numpy as jnp
from jax import lax
from jax.experimental import pallas as pl
from jax.experimental.pallas import tpu as pltpu
from jax.sharding import PartitionSpec as P

HD = 96
W = 1024
SINKS = 4
G = 2
RING = 16
BLK = 128
QB = 256
CH = 256
LANES = 128
FAR = 1 << 28
LOW = -1e30


def pack_kernel(head, q_ref, k_ref, v_ref, ck_ref, cv_ref, sk_ref, sv_ref, out_ref, sink_ref):
    heads = q_ref.shape[1] // HD
    for which, ref in enumerate((q_ref, k_ref, v_ref)):
        turned = ref[...].T
        for p in range(heads):
            out_ref[p, which * HD : (which + 1) * HD, :] = turned[p * HD : (p + 1) * HD, :]
    rows = ck_ref.shape[0]
    fill = jnp.zeros((rows, LANES - HD), ck_ref.dtype)
    for which, ref in enumerate((ck_ref, cv_ref)):
        for p in range(heads):
            piece = jnp.concatenate([ref[:, p * HD : (p + 1) * HD], fill], axis=1)
            base = 3 * HD + which * rows
            out_ref[p, base : base + rows, :] = piece
    width = sk_ref.shape[1]
    column = lax.broadcasted_iota(jnp.int32, (width, LANES), 0)
    lane = lax.broadcasted_iota(jnp.int32, (width, LANES), 1)
    pick = ((column == head[0] * HD + lane) & (lane < HD)).astype(jnp.float32).astype(jnp.bfloat16)
    for which, ref in enumerate((sk_ref, sv_ref)):
        piece = jnp.dot(ref[...], pick, preferred_element_type=jnp.float32)
        piece = jnp.concatenate([piece, jnp.zeros_like(piece)], axis=0)
        sink_ref[which * 16 : (which + 1) * 16, :] = piece.astype(jnp.bfloat16)


def attend_kernel(
    place, lengths, groups, sink_ref, own_ref, win_ref, *rest, rings
):
    caches = rest[: rings]
    out_ref, key_ref, val_ref, low_ref, need = rest[rings:]
    ring = place[0]
    base = ring * RING * BLK
    front = W
    own = RING * BLK
    cache_at = front + own
    blocks = own // QB
    factor = (1.0 / math.sqrt(HD)) * math.log2(math.e)
    pad = jnp.zeros((LANES - HD, BLK), jnp.bfloat16)

    def turn(piece):
        return jnp.concatenate([piece, pad], axis=0).T

    for j in range(RING // 2):
        key_ref[j * BLK : (j + 1) * BLK, :] = turn(win_ref[j, 0:HD, :])
        val_ref[j] = win_ref[j, HD : 2 * HD, :]
    for j in range(RING):
        at = front + j * BLK
        key_ref[at : at + BLK, :] = turn(own_ref[j, HD : 2 * HD, :])
        val_ref[front // BLK + j] = own_ref[j, 2 * HD : 3 * HD, :]
    rows = RING * 16
    for k in range(rings):
        x_lo = (ring // 4 + k // 4) % 2
        y = (ring % 4 + k % 4) % 4
        source = lax.rem(lax.rem(ring, 4) + 4 - k % 4, 4) + 4 * lax.rem(ring // 4 + k // 4, 2)
        piece = caches[k][...]
        keys = piece[:, 0:16, :].reshape(rows, LANES)
        vals = piece[:, 16:32, :].reshape(rows, LANES)
        at = pl.multiple_of(cache_at + source * rows, rows)
        key_ref[pl.ds(at, rows), :] = keys
        turned = vals.T
        for half in range(rows // BLK):
            val_ref[cache_at // BLK + source * (rows // BLK) + half] = turned[
                0:HD, half * BLK : (half + 1) * BLK
            ]

    for b in range(blocks):
        need[b] = FAR
        need[blocks + b] = FAR
        need[2 * blocks + b] = FAR

    def one_request(r, carry):
        start, start_col, group_col = carry
        length = lengths[r]
        group = groups[r]
        first = jnp.maximum((start - base) // QB, 0)
        last = jnp.minimum((start + length - 1 - base) // QB, blocks - 1)
        first = jnp.where(start < base, 0, first)

        def mark(b, _):
            need[b] = jnp.minimum(need[b], start)
            offset = jnp.maximum(base + b * QB - start, 0)
            at = (1 + group) * blocks + b
            need[at] = jnp.minimum(need[at], offset)
            return 0

        @pl.when((start < base + own) & (start + length > base))
        def _():
            lax.fori_loop(first, last + 1, mark, 0)

        row = lax.broadcasted_iota(jnp.int32, start_col.shape, 0)
        start_col = jnp.where(row == r, start, start_col)
        group_col = jnp.where(row == r, group, group_col)
        return (start + length, start_col, group_col)

    reqs = lengths.shape[0]
    column = jnp.zeros((reqs, QB), jnp.int32)
    _, start_col, group_col = lax.fori_loop(0, reqs, one_request, (jnp.int32(0), column, column))

    lane = lax.broadcasted_iota(jnp.int32, (1, QB), 1)
    row_iota = lax.broadcasted_iota(jnp.int32, (CH, QB), 0)
    sink_row = lax.broadcasted_iota(jnp.int32, (16, QB), 0)

    def dot(a, b):
        return jnp.dot(a, b, preferred_element_type=jnp.float32)

    def one_block(b, _):
        index = base + b * QB + lane
        begun = start_col <= index
        start_q = jnp.max(jnp.where(begun, start_col, 0), axis=0, keepdims=True)
        here = begun & (start_col == start_q)
        group_q = jnp.max(jnp.where(here, group_col, 0), axis=0, keepdims=True)
        offset = index - start_q
        low_suffix = jnp.maximum(start_q, index - (W - 1)) - base + front
        low_ref[0] = jnp.broadcast_to(low_suffix, (8, QB))
        for g in range(G):
            low_g = jnp.where(group_q == g, cache_at + g * W + offset + 1, FAR)
            low_ref[1 + g] = jnp.broadcast_to(low_g, (8, QB))
        low_ref[1 + G] = jnp.full((8, QB), FAR, jnp.int32)
        q_t = jnp.concatenate([own_ref[2 * b, 0:HD, :], own_ref[2 * b + 1, 0:HD, :]], axis=1)
        q_t = jnp.concatenate([q_t, jnp.zeros((LANES - HD, QB), jnp.bfloat16)], axis=0)

        def values(at):
            slot = at // BLK
            return jnp.concatenate([val_ref[slot], val_ref[slot + 1]], axis=1)

        at0 = pl.multiple_of(front + b * QB, CH)
        s_d = dot(key_ref[pl.ds(at0, CH), :], q_t)
        key_at = row_iota + at0
        s_d = jnp.where((key_at >= low_suffix) & (key_at <= at0 + lane), s_d, LOW)
        s_s = dot(sink_ref[0:16, :], q_t)
        s_s = jnp.where((sink_row // SINKS == group_q) & (sink_row < G * SINKS), s_s, LOW)
        top = jnp.maximum(jnp.max(s_d, axis=0, keepdims=True), jnp.max(s_s, axis=0, keepdims=True))
        p_d = jnp.exp2((s_d - top) * factor)
        p_s = jnp.exp2((s_s - top) * factor)
        den = jnp.sum(p_d, axis=0, keepdims=True) + jnp.sum(p_s, axis=0, keepdims=True)
        sink_v = sink_ref[16:32, :].T[0:HD, :]
        acc = dot(values(at0), p_d.astype(jnp.bfloat16)) + dot(sink_v, p_s.astype(jnp.bfloat16))

        first = jnp.maximum(need[b], base + b * QB - (W - 1)) - base + front
        n_suffix = front // CH + b - first // CH
        c0 = [jnp.minimum((need[(1 + g) * blocks + b] + 1) // CH, W // CH) for g in range(G)]
        n0, n1 = [W // CH - c for c in c0]
        total = n_suffix + n0 + n1

        def where_is(j):
            in0 = j - n_suffix
            in1 = in0 - n0
            at = jnp.where(
                in0 < 0,
                (first // CH + j) * CH,
                jnp.where(
                    in1 < 0,
                    cache_at + (c0[0] + in0) * CH,
                    jnp.where(j < total, cache_at + W + (c0[1] + in1) * CH, 0),
                ),
            )
            kind = jnp.where(in0 < 0, 0, jnp.where(in1 < 0, 1, jnp.where(j < total, 2, 3)))
            return pl.multiple_of(at, CH), kind

        def step(j, state):
            top, den, acc = state
            scores, ats = [], []
            for u in range(2):
                at, kind = where_is(2 * j + u)
                s = dot(key_ref[pl.ds(at, CH), :], q_t)
                low = low_ref[kind][0:1, :]
                scores.append(jnp.where(row_iota + at >= low, s, LOW))
                ats.append(at)
            new = jnp.maximum(
                jnp.max(scores[0], axis=0, keepdims=True), jnp.max(scores[1], axis=0, keepdims=True)
            )
            new = jnp.maximum(top, new)
            fade = jnp.exp2((top - new) * factor)
            den = den * fade
            acc = acc * fade
            for u in range(2):
                p = jnp.exp2((scores[u] - new) * factor)
                den = den + jnp.sum(p, axis=0, keepdims=True)
                acc = acc + dot(values(ats[u]), p.astype(jnp.bfloat16))
            return (new, den, acc)

        top, den, acc = lax.fori_loop(0, (total + 1) // 2, step, (top, den, acc))
        done = (acc / den).astype(jnp.bfloat16)
        out_ref[2 * b] = done[:, 0:BLK]
        out_ref[2 * b + 1] = done[:, BLK:QB]
        return 0

    lax.fori_loop(0, blocks, one_block, 0)


def vmem():
    return pl.BlockSpec(memory_space=pltpu.VMEM)


def smem():
    return pl.BlockSpec(memory_space=pltpu.SMEM)


def shards(
    queries, keys, values, cache_k, cache_v, sink_k, sink_v, suffix_lengths, request_group, w_out
):
    rows, width = queries.shape
    heads = width // HD
    seq = lax.axis_size("seq")
    rings = seq // RING
    device = lax.axis_index("seq")
    half = lax.axis_index("head")
    chunk = 3 * HD + 32
    packed, sinks = pl.pallas_call(
        pack_kernel,
        out_shape=(
            jax.ShapeDtypeStruct((heads, chunk, LANES), jnp.bfloat16),
            jax.ShapeDtypeStruct((32, LANES), jnp.bfloat16),
        ),
        in_specs=[smem()] + [vmem()] * 7,
        out_specs=(vmem(), vmem()),
        name="pack",
    )(
        (device % RING).reshape(1), queries, keys, values, cache_k, cache_v, sink_k, sink_v
    )
    members = [[r * RING + i for i in range(RING)] for r in range(rings)]
    mine = lax.all_to_all(packed, "seq", 0, 0, axis_index_groups=members, tiled=True)
    cache = mine[:, 3 * HD :, :]

    def ring_after(r, k):
        return (r % 4 + k % 4) % 4 + 4 * ((r // 4 + k // 4) % 2)

    caches = [cache]
    for k in range(1, rings):
        pairs = [
            (r * RING + i, ring_after(r, k) * RING + i) for r in range(rings) for i in range(RING)
        ]
        caches.append(lax.ppermute(cache, "seq", pairs))
    window = lax.ppermute(
        mine[RING // 2 :, HD : 3 * HD, :], "seq", [(s, s + RING) for s in range(seq - RING)]
    )
    attn = pl.pallas_call(
        functools.partial(attend_kernel, rings=rings),
        out_shape=jax.ShapeDtypeStruct((RING, HD, BLK), jnp.bfloat16),
        in_specs=[smem()] * 3 + [vmem()] * (3 + rings),
        out_specs=vmem(),
        scratch_shapes=[
            pltpu.VMEM((W + RING * BLK + G * W, LANES), jnp.bfloat16),
            pltpu.VMEM(((W + RING * BLK + G * W) // BLK, HD, BLK), jnp.bfloat16),
            pltpu.VMEM((2 + G, 8, QB), jnp.int32),
            pltpu.SMEM((3 * RING * BLK // QB,), jnp.int32),
        ],
        name="attend",
    )((device // RING).reshape(1), suffix_lengths, request_group, sinks, mine, window, *caches)
    back = lax.all_to_all(attn, "seq", 0, 0, axis_index_groups=members, tiled=True)
    attn_t = back.reshape(width, rows)
    full = jnp.einsum("cd,cs->ds", w_out, attn_t, preferred_element_type=jnp.float32)
    features = full.shape[0] // 2
    keep = lax.dynamic_slice_in_dim(full, half * features, features, 0)
    give = lax.dynamic_slice_in_dim(full, (1 - half) * features, features, 0)
    got = lax.ppermute(give.astype(jnp.bfloat16), "head", [(0, 1), (1, 0)])
    return (keep + got.astype(jnp.float32)).astype(jnp.bfloat16)


def solution(mesh):
    placed = (
        P("seq", "head"),
        P("seq", "head"),
        P("seq", "head"),
        P("seq", "head"),
        P("seq", "head"),
        P(None, "head"),
        P(None, "head"),
        P(),
        P(),
        P("head", None),
    )
    return jax.shard_map(
        shards, mesh=mesh, in_specs=placed, out_specs=P("head", "seq"), check_vma=False
    )
```

```python
import functools
import math

import jax
import jax.numpy as jnp
from jax import lax
from jax.experimental import pallas as pl
from jax.experimental.pallas import tpu as pltpu
from jax.sharding import PartitionSpec as P

HD = 96
W = 1024
SINKS = 4
G = 2
RING = 16
BLK = 128
QB = 256
CH = 256
LANES = 128
FAR = 1 << 28
LOW = -1e30
VMEM_LIMIT = 24 << 20


def pack_kernel(head, q_ref, k_ref, v_ref, ck_ref, cv_ref, sk_ref, sv_ref, query_ref, out_ref, sink_ref):
    heads = q_ref.shape[1] // HD
    for which, ref in enumerate((k_ref, v_ref, q_ref)):
        turned = ref[...].T
        for p in range(heads):
            piece = turned[p * HD : (p + 1) * HD, :]
            if which == 2:
                query_ref[p] = piece
            else:
                out_ref[p, which * HD : (which + 1) * HD, :] = piece
    rows = ck_ref.shape[0]
    fill = jnp.zeros((rows, LANES - HD), ck_ref.dtype)
    for which, ref in enumerate((ck_ref, cv_ref)):
        for p in range(heads):
            piece = jnp.concatenate([ref[:, p * HD : (p + 1) * HD], fill], axis=1)
            base = 2 * HD + which * rows
            out_ref[p, base : base + rows, :] = piece
    width = sk_ref.shape[1]
    column = lax.broadcasted_iota(jnp.int32, (width, LANES), 0)
    lane = lax.broadcasted_iota(jnp.int32, (width, LANES), 1)
    pick = ((column == head[0] * HD + lane) & (lane < HD)).astype(jnp.float32).astype(jnp.bfloat16)
    for which, ref in enumerate((sk_ref, sv_ref)):
        piece = jnp.dot(ref[...], pick, preferred_element_type=jnp.float32)
        piece = jnp.concatenate([piece, jnp.zeros_like(piece)], axis=0)
        sink_ref[which * 16 : (which + 1) * 16, :] = piece.astype(jnp.bfloat16)


def gather_facts(place, lengths, groups, need, blocks):
    base = place[0] * RING * BLK
    own = RING * BLK
    for b in range((1 + G) * blocks):
        need[b] = FAR

    def one_request(r, carry):
        start, start_col, group_col = carry
        length = lengths[r]
        group = groups[r]
        first = jnp.where(start < base, 0, (start - base) // QB)
        last = jnp.minimum((start + length - 1 - base) // QB, blocks - 1)

        def mark(b, _):
            need[b] = jnp.minimum(need[b], start)
            offset = jnp.maximum(base + b * QB - start, 0)
            at = (1 + group) * blocks + b
            need[at] = jnp.minimum(need[at], offset)
            return 0

        @pl.when((start < base + own) & (start + length > base))
        def _():
            lax.fori_loop(first, last + 1, mark, 0)

        row = lax.broadcasted_iota(jnp.int32, start_col.shape, 0)
        start_col = jnp.where(row == r, start, start_col)
        group_col = jnp.where(row == r, group, group_col)
        return (start + length, start_col, group_col)

    reqs = lengths.shape[0]
    column = jnp.zeros((reqs, QB), jnp.int32)
    _, start_col, group_col = lax.fori_loop(0, reqs, one_request, (jnp.int32(0), column, column))
    return base, start_col, group_col


def query_facts(index, start_col, group_col):
    begun = start_col <= index
    start_q = jnp.max(jnp.where(begun, start_col, 0), axis=0, keepdims=True)
    here = begun & (start_col == start_q)
    group_q = jnp.max(jnp.where(here, group_col, 0), axis=0, keepdims=True)
    return jnp.maximum(start_q, index - (W - 1)), index - start_q, group_q


def turn(piece):
    pad = jnp.zeros((LANES - HD, BLK), jnp.bfloat16)
    return jnp.concatenate([piece, pad], axis=0).T


def query_block(query_ref, b):
    q_t = jnp.concatenate([query_ref[2 * b], query_ref[2 * b + 1]], axis=1)
    return jnp.concatenate([q_t, jnp.zeros((LANES - HD, QB), jnp.bfloat16)], axis=0)


def values(val_ref, at):
    slot = at // BLK
    return jnp.concatenate([val_ref[slot], val_ref[slot + 1]], axis=1)


def dot(a, b):
    return jnp.dot(a, b, preferred_element_type=jnp.float32)


FACTOR = (1.0 / math.sqrt(HD)) * math.log2(math.e)


def prep_kernel(place, lengths, groups, own_ref, key_ref, low_ref, need):
    for j in range(RING):
        key_ref[j * BLK : (j + 1) * BLK, :] = turn(own_ref[j, 0:HD, :])
    own = RING * BLK
    blocks = own // QB
    cache_at = W + own
    base, start_col, group_col = gather_facts(place, lengths, groups, need, blocks)
    lane = lax.broadcasted_iota(jnp.int32, (1, QB), 1)
    for b in range(blocks):
        index = base + b * QB + lane
        low_q, offset, group_q = query_facts(index, start_col, group_col)
        low_ref[b, 0:1, :] = low_q - base + W
        for g in range(G):
            low_ref[b, 1 + g : 2 + g, :] = jnp.where(
                group_q == g, cache_at + g * W + offset + 1, FAR
            )
        low_ref[b, 1 + G : 2 + G, :] = jnp.full((1, QB), FAR, jnp.int32)
        low_ref[b, 2 + G : 3 + G, :] = group_q


def attend_kernel(
    place, need, low_ref, sink_ref, query_ref, own_ref, turned_ref, win_ref, *rest, rings
):
    caches = rest[:rings]
    out_ref, key_ref, val_ref = rest[rings:]
    ring = place[0]
    base = ring * RING * BLK
    front = W
    own = RING * BLK
    cache_at = front + own
    blocks = own // QB
    for j in range(RING // 2):
        key_ref[j * BLK : (j + 1) * BLK, :] = turn(win_ref[j, 0:HD, :])
        val_ref[j] = win_ref[j, HD : 2 * HD, :]
    key_ref[front : front + own, :] = turned_ref[...]
    for j in range(RING):
        val_ref[front // BLK + j] = own_ref[j, HD : 2 * HD, :]
    rows = RING * 16
    for k in range(rings):
        source = lax.rem(lax.rem(ring, 4) + k % 4, 4) + 4 * lax.rem(ring // 4 + k // 4, 2)
        piece = caches[k][...]
        at = pl.multiple_of(cache_at + source * rows, rows)
        key_ref[pl.ds(at, rows), :] = piece[:, 0:16, :].reshape(rows, LANES)
        turned = piece[:, 16:32, :].reshape(rows, LANES).T
        for half in range(rows // BLK):
            val_ref[at // BLK + half] = turned[0:HD, half * BLK : (half + 1) * BLK]
    lane = lax.broadcasted_iota(jnp.int32, (1, QB), 1)
    row_iota = lax.broadcasted_iota(jnp.int32, (CH, QB), 0)
    sink_row = lax.broadcasted_iota(jnp.int32, (16, QB), 0)
    sink_v = sink_ref[16:32, :].T[0:HD, :]

    def one_block(b, _):
        low_suffix = low_ref[b, 0:1, :]
        group_q = low_ref[b, 2 + G : 3 + G, :]
        q_t = query_block(query_ref, b)
        at0 = pl.multiple_of(front + b * QB, CH)
        s_d = dot(key_ref[pl.ds(at0, CH), :], q_t)
        s_d = jnp.where((row_iota >= low_suffix - at0) & (row_iota <= lane), s_d, LOW)
        s_s = dot(sink_ref[0:16, :], q_t)
        s_s = jnp.where((sink_row // SINKS == group_q) & (sink_row < G * SINKS), s_s, LOW)
        top = jnp.maximum(jnp.max(s_d, axis=0, keepdims=True), jnp.max(s_s, axis=0, keepdims=True))
        p_d = jnp.exp2((s_d - top) * FACTOR)
        p_s = jnp.exp2((s_s - top) * FACTOR)
        den = jnp.sum(p_d, axis=0, keepdims=True) + jnp.sum(p_s, axis=0, keepdims=True)
        acc = dot(values(val_ref, at0), p_d.astype(jnp.bfloat16))
        acc = acc + dot(sink_v, p_s.astype(jnp.bfloat16))

        first = (jnp.maximum(need[b] - base, b * QB - (W - 1)) + front) // CH
        n_suffix = front // CH + b - first
        c0 = [jnp.minimum((need[(1 + g) * blocks + b] + 1) // CH, W // CH) for g in range(G)]
        n0, n1 = [W // CH - c for c in c0]
        total = n_suffix + n0 + n1

        def where_is(j):
            in0 = j - n_suffix
            in1 = in0 - n0
            at = jnp.where(
                in0 < 0,
                (first + j) * CH,
                jnp.where(
                    in1 < 0,
                    cache_at + (c0[0] + in0) * CH,
                    jnp.where(j < total, cache_at + W + (c0[1] + in1) * CH, 0),
                ),
            )
            kind = jnp.where(in0 < 0, 0, jnp.where(in1 < 0, 1, jnp.where(j < total, 2, 3)))
            return pl.multiple_of(at, CH), kind

        def step(j, state):
            top, den, acc = state
            scores, ats = [], []
            for u in range(2):
                at, kind = where_is(2 * j + u)
                s = dot(key_ref[pl.ds(at, CH), :], q_t)
                low = low_ref[b, pl.ds(kind, 1), :] - at
                scores.append(jnp.where(row_iota >= low, s, LOW))
                ats.append(at)
            new = jnp.maximum(
                jnp.max(scores[0], axis=0, keepdims=True),
                jnp.max(scores[1], axis=0, keepdims=True),
            )
            new = jnp.maximum(top, new)
            fade = jnp.exp2((top - new) * FACTOR)
            den = den * fade
            ps = []
            for u in range(2):
                p = jnp.exp2((scores[u] - new) * FACTOR)
                den = den + jnp.sum(p, axis=0, keepdims=True)
                ps.append(p.astype(jnp.bfloat16))
            vals = jnp.concatenate([values(val_ref, at) for at in ats], axis=1)
            acc = acc * fade + dot(vals, jnp.concatenate(ps, axis=0))
            return (new, den, acc)

        _, den, acc = lax.fori_loop(0, (total + 1) // 2, step, (top, den, acc))
        done = (acc / den).astype(jnp.bfloat16)
        out_ref[2 * b] = done[:, 0:BLK]
        out_ref[2 * b + 1] = done[:, BLK:QB]
        return 0

    lax.fori_loop(0, blocks, one_block, 0)


def project_here_kernel(side, attn_ref, w_ref, out_ref, half_ref, arrived):
    features = half_ref.shape[1]
    columns = pl.ds(pl.multiple_of(side[0] * features, features), features)
    parts = arrived.shape[0]
    tall = half_ref.shape[0] // parts
    loads = [
        pltpu.make_async_copy(
            w_ref.at[pl.ds(n * tall, tall), columns],
            half_ref.at[pl.ds(n * tall, tall), :],
            arrived.at[n],
        )
        for n in range(parts)
    ]
    for load in loads:
        load.start()
    turned = attn_ref[...].T
    for load in loads:
        load.wait()
    piece = 256
    for j in range(features // piece):
        at = slice(j * piece, (j + 1) * piece)
        out_ref[at, :] = dot(turned, half_ref[:, at]).T.astype(out_ref.dtype)


def project_kernel(side, attn_ref, w_ref, out_ref, turned_ref):
    @pl.when(pl.program_id(0) == 0)
    def _():
        turned_ref[...] = attn_ref[...].T

    out_ref[...] = dot(turned_ref[...], w_ref[...]).T.astype(out_ref.dtype)


def project_cost(width, features, rows):
    return pl.CostEstimate(
        flops=2 * width * features * rows, bytes_accessed=2 * width * features, transcendentals=0
    )


def project_here(side, attn_t, w_out):
    width, rows = attn_t.shape
    features = w_out.shape[1] // 2
    return pl.pallas_call(
        project_here_kernel,
        out_shape=jax.ShapeDtypeStruct((features, rows), jnp.bfloat16),
        in_specs=[smem(), vmem(), pl.BlockSpec(memory_space=pltpu.HBM)],
        out_specs=vmem(),
        scratch_shapes=[
            pltpu.VMEM((width, features), jnp.bfloat16),
            pltpu.SemaphoreType.DMA((12,)),
        ],
        cost_estimate=project_cost(width, features, rows),
        compiler_params=pltpu.CompilerParams(vmem_limit_bytes=VMEM_LIMIT),
        name="project_here",
    )(side.reshape(1), attn_t, w_out)


def project(side, attn_t, w_out):
    width, rows = attn_t.shape
    features = w_out.shape[1] // 2
    piece = 512
    steps = features // piece
    return pl.pallas_call(
        project_kernel,
        out_shape=jax.ShapeDtypeStruct((features, rows), jnp.float32),
        grid_spec=pltpu.PrefetchScalarGridSpec(
            num_scalar_prefetch=1,
            grid=(steps,),
            in_specs=[
                pl.BlockSpec((width, rows), lambda j, side: (0, 0)),
                pl.BlockSpec((width, piece), lambda j, side: (0, side[0] * steps + j)),
            ],
            out_specs=pl.BlockSpec((piece, rows), lambda j, side: (j, 0)),
            scratch_shapes=[pltpu.VMEM((rows, width), jnp.bfloat16)],
        ),
        cost_estimate=project_cost(width, features, rows),
        name="project",
    )(side.reshape(1), attn_t, w_out)


def vmem():
    return pl.BlockSpec(memory_space=pltpu.VMEM)


def smem():
    return pl.BlockSpec(memory_space=pltpu.SMEM)


def shards(
    queries, keys, values, cache_k, cache_v, sink_k, sink_v, suffix_lengths, request_group, w_out
):
    rows, width = queries.shape
    heads = width // HD
    seq = lax.axis_size("seq")
    rings = seq // RING
    device = lax.axis_index("seq")
    half = lax.axis_index("head")
    packed_q, packed, sinks = pl.pallas_call(
        pack_kernel,
        out_shape=(
            jax.ShapeDtypeStruct((heads, HD, LANES), jnp.bfloat16),
            jax.ShapeDtypeStruct((heads, 2 * HD + 32, LANES), jnp.bfloat16),
            jax.ShapeDtypeStruct((32, LANES), jnp.bfloat16),
        ),
        in_specs=[smem()] + [vmem()] * 7,
        out_specs=(vmem(), vmem(), vmem()),
        name="pack",
    )(
        (device % RING).reshape(1), queries, keys, values, cache_k, cache_v, sink_k, sink_v
    )
    members = [[r * RING + i for i in range(RING)] for r in range(rings)]

    def trade(array, groups):
        return lax.all_to_all(array, "seq", 0, 0, axis_index_groups=groups, tiled=True)

    mine = trade(packed, members)
    mine_q = trade(packed_q, members)
    window = lax.ppermute(
        mine[RING // 2 :, : 2 * HD, :], "seq", [(s, s + RING) for s in range(seq - RING)]
    )
    cache = mine[:, 2 * HD :, :]

    def send(array, dx, dy):
        pairs = []
        for r in range(rings):
            to = (r % 4 + dy) % 4 + 4 * ((r // 4 + dx) % 2)
            pairs += [(r * RING + i, to * RING + i) for i in range(RING)]
        return lax.ppermute(array, "seq", pairs)

    near_y = send(cache, 0, 3)
    near_x = send(cache, 1, 0)
    back_y = send(cache, 0, 1)
    far_y = send(near_y, 0, 3)
    near_xy = send(near_x, 0, 3)
    back_xy = send(back_y, 1, 0)
    far_xy = send(far_y, 1, 0)
    caches = [cache, near_y, far_y, back_y, near_x, near_xy, far_xy, back_xy]
    own = RING * BLK
    blocks = own // QB
    total = W + own + G * W
    place = (device // RING).reshape(1)
    turned, lows, need = pl.pallas_call(
        prep_kernel,
        out_shape=(
            jax.ShapeDtypeStruct((own, LANES), jnp.bfloat16),
            jax.ShapeDtypeStruct((blocks, 8, QB), jnp.int32),
            jax.ShapeDtypeStruct(((1 + G) * blocks,), jnp.int32),
        ),
        in_specs=[smem()] * 3 + [vmem()],
        out_specs=(vmem(), vmem(), smem()),
        cost_estimate=pl.CostEstimate(
            flops=1 << 20, bytes_accessed=1 << 22, transcendentals=0
        ),
        compiler_params=pltpu.CompilerParams(vmem_limit_bytes=VMEM_LIMIT),
        name="prep",
    )(place, suffix_lengths, request_group, mine)
    attn = pl.pallas_call(
        functools.partial(attend_kernel, rings=rings),
        out_shape=jax.ShapeDtypeStruct((RING, HD, BLK), jnp.bfloat16),
        in_specs=[smem()] * 2 + [vmem()] * (6 + rings),
        out_specs=vmem(),
        scratch_shapes=[
            pltpu.VMEM((total, LANES), jnp.bfloat16),
            pltpu.VMEM((total // BLK, HD, BLK), jnp.bfloat16),
        ],
        compiler_params=pltpu.CompilerParams(vmem_limit_bytes=VMEM_LIMIT),
        name="attend",
    )(place, need, lows, sinks, mine_q, mine, turned, window, *caches)
    attn_t = trade(attn, members).reshape(width, rows)
    give = project_here(1 - half, attn_t, w_out)
    got = lax.ppermute(give, "head", [(0, 1), (1, 0)])
    keep = project(half, attn_t, w_out)
    return (keep + got.astype(jnp.float32)).astype(jnp.bfloat16)


def solution(mesh):
    placed = (
        P("seq", "head"),
        P("seq", "head"),
        P("seq", "head"),
        P("seq", "head"),
        P("seq", "head"),
        P(None, "head"),
        P(None, "head"),
        P(),
        P(),
        P("head", None),
    )
    return jax.shard_map(
        shards, mesh=mesh, in_specs=placed, out_specs=P("head", "seq"), check_vma=False
    )
```

```python
import functools
import math

import jax
import jax.numpy as jnp
from jax import lax
from jax.experimental import pallas as pl
from jax.experimental.pallas import tpu as pltpu
from jax.sharding import PartitionSpec as P

HD = 96
W = 1024
SINKS = 4
G = 2
RING = 16
BLK = 128
QB = 256
CH = 256
LANES = 128
FAR = 1 << 28
LOW = -1e30
VMEM_LIMIT = 24 << 20


def pack_kernel(k_ref, v_ref, ck_ref, cv_ref, out_ref):
    heads = k_ref.shape[1] // HD
    for which, ref in enumerate((k_ref, v_ref)):
        turned = ref[...].T
        for p in range(heads):
            out_ref[p, which * HD : (which + 1) * HD, :] = turned[p * HD : (p + 1) * HD, :]
    rows = ck_ref.shape[0]
    fill = jnp.zeros((rows, LANES - HD), ck_ref.dtype)
    for which, ref in enumerate((ck_ref, cv_ref)):
        for p in range(heads):
            piece = jnp.concatenate([ref[:, p * HD : (p + 1) * HD], fill], axis=1)
            base = 2 * HD + which * rows
            out_ref[p, base : base + rows, :] = piece


def pack_query_kernel(head, q_ref, sk_ref, sv_ref, query_ref, sink_ref):
    turned = q_ref[...].T
    for p in range(q_ref.shape[1] // HD):
        query_ref[p] = turned[p * HD : (p + 1) * HD, :]
    width = sk_ref.shape[1]
    column = lax.broadcasted_iota(jnp.int32, (width, LANES), 0)
    lane = lax.broadcasted_iota(jnp.int32, (width, LANES), 1)
    pick = ((column == head[0] * HD + lane) & (lane < HD)).astype(jnp.float32).astype(jnp.bfloat16)
    for which, ref in enumerate((sk_ref, sv_ref)):
        piece = jnp.dot(ref[...], pick, preferred_element_type=jnp.float32)
        piece = jnp.concatenate([piece, jnp.zeros_like(piece)], axis=0)
        sink_ref[which * 16 : (which + 1) * 16, :] = piece.astype(jnp.bfloat16)


def gather_facts(place, lengths, groups, need, blocks):
    base = place[0] * RING * BLK
    own = RING * BLK
    for b in range((1 + G) * blocks):
        need[b] = FAR

    def one_request(r, carry):
        start, start_col, group_col = carry
        length = lengths[r]
        group = groups[r]
        first = jnp.where(start < base, 0, (start - base) // QB)
        last = jnp.minimum((start + length - 1 - base) // QB, blocks - 1)

        def mark(b, _):
            need[b] = jnp.minimum(need[b], start)
            offset = jnp.maximum(base + b * QB - start, 0)
            at = (1 + group) * blocks + b
            need[at] = jnp.minimum(need[at], offset)
            return 0

        @pl.when((start < base + own) & (start + length > base))
        def _():
            lax.fori_loop(first, last + 1, mark, 0)

        row = lax.broadcasted_iota(jnp.int32, start_col.shape, 0)
        start_col = jnp.where(row == r, start, start_col)
        group_col = jnp.where(row == r, group, group_col)
        return (start + length, start_col, group_col)

    reqs = lengths.shape[0]
    column = jnp.zeros((reqs, QB), jnp.int32)
    _, start_col, group_col = lax.fori_loop(0, reqs, one_request, (jnp.int32(0), column, column))
    return base, start_col, group_col


def query_facts(index, start_col, group_col):
    begun = start_col <= index
    start_q = jnp.max(jnp.where(begun, start_col, 0), axis=0, keepdims=True)
    here = begun & (start_col == start_q)
    group_q = jnp.max(jnp.where(here, group_col, 0), axis=0, keepdims=True)
    return jnp.maximum(start_q, index - (W - 1)), index - start_q, group_q


def turn(piece):
    pad = jnp.zeros((LANES - HD, BLK), jnp.bfloat16)
    return jnp.concatenate([piece, pad], axis=0).T


def query_block(query_ref, b):
    q_t = jnp.concatenate([query_ref[2 * b], query_ref[2 * b + 1]], axis=1)
    return jnp.concatenate([q_t, jnp.zeros((LANES - HD, QB), jnp.bfloat16)], axis=0)


def values(val_ref, at):
    slot = at // BLK
    return jnp.concatenate([val_ref[slot], val_ref[slot + 1]], axis=1)


def dot(a, b):
    return jnp.dot(a, b, preferred_element_type=jnp.float32)


FACTOR = (1.0 / math.sqrt(HD)) * math.log2(math.e)


def prep_kernel(place, lengths, groups, own_ref, key_ref, low_ref, need):
    for j in range(RING):
        key_ref[j * BLK : (j + 1) * BLK, :] = turn(own_ref[j, 0:HD, :])
    own = RING * BLK
    blocks = own // QB
    cache_at = own
    base, start_col, group_col = gather_facts(place, lengths, groups, need, blocks)
    lane = lax.broadcasted_iota(jnp.int32, (1, QB), 1)
    for b in range(blocks):
        index = base + b * QB + lane
        low_q, offset, group_q = query_facts(index, start_col, group_col)
        low_ref[b, 0:1, :] = low_q - base
        for g in range(G):
            low_ref[b, 1 + g : 2 + g, :] = jnp.where(
                group_q == g, cache_at + g * W + offset + 1, FAR
            )
        low_ref[b, 1 + G : 2 + G, :] = jnp.full((1, QB), FAR, jnp.int32)
        low_ref[b, 2 + G : 3 + G, :] = group_q


def visit(total, where_is, key_ref, val_ref, low_of, q_t, state):
    row_iota = lax.broadcasted_iota(jnp.int32, (CH, QB), 0)

    def step(j, state):
        top, den, acc = state
        scores, ats = [], []
        for u in range(2):
            at, kind = where_is(2 * j + u)
            s = dot(key_ref[pl.ds(at, CH), :], q_t)
            scores.append(jnp.where(row_iota >= low_of(kind) - at, s, LOW))
            ats.append(at)
        new = jnp.maximum(
            jnp.max(scores[0], axis=0, keepdims=True), jnp.max(scores[1], axis=0, keepdims=True)
        )
        new = jnp.maximum(top, new)
        fade = jnp.exp2((top - new) * FACTOR)
        den = den * fade
        ps = []
        for u in range(2):
            p = jnp.exp2((scores[u] - new) * FACTOR)
            den = den + jnp.sum(p, axis=0, keepdims=True)
            ps.append(p.astype(jnp.bfloat16))
        vals = jnp.concatenate([values(val_ref, at) for at in ats], axis=1)
        acc = acc * fade + dot(vals, jnp.concatenate(ps, axis=0))
        return (new, den, acc)

    return lax.fori_loop(0, (total + 1) // 2, step, state)


def attend_kernel(
    place, need, low_ref, sink_ref, query_ref, own_ref, turned_ref, *rest, rings
):
    caches = rest[:rings]
    upper_ref, stat_ref, acc_ref, key_ref, val_ref = rest[rings:]
    ring = place[0]
    base = ring * RING * BLK
    own = RING * BLK
    blocks = own // QB
    key_ref[0:own, :] = turned_ref[...]
    for j in range(RING):
        val_ref[j] = own_ref[j, HD : 2 * HD, :]
    rows = RING * 16
    for k in range(rings):
        source = lax.rem(lax.rem(ring, 4) + k % 4, 4) + 4 * lax.rem(ring // 4 + k // 4, 2)
        piece = caches[k][...]
        at = pl.multiple_of(own + source * rows, rows)
        key_ref[pl.ds(at, rows), :] = piece[:, 0:16, :].reshape(rows, LANES)
        turned = piece[:, 16:32, :].reshape(rows, LANES).T
        for half in range(rows // BLK):
            val_ref[at // BLK + half] = turned[0:HD, half * BLK : (half + 1) * BLK]
    lane = lax.broadcasted_iota(jnp.int32, (1, QB), 1)
    row_iota = lax.broadcasted_iota(jnp.int32, (CH, QB), 0)
    sink_row = lax.broadcasted_iota(jnp.int32, (16, QB), 0)
    sink_v = sink_ref[16:32, :].T[0:HD, :]

    def one_block(b, _):
        low_suffix = low_ref[b, 0:1, :]
        group_q = low_ref[b, 2 + G : 3 + G, :]
        q_t = query_block(query_ref, b)
        at0 = pl.multiple_of(b * QB, CH)
        s_d = dot(key_ref[pl.ds(at0, CH), :], q_t)
        s_d = jnp.where((row_iota >= low_suffix - at0) & (row_iota <= lane), s_d, LOW)
        s_s = dot(sink_ref[0:16, :], q_t)
        s_s = jnp.where((sink_row // SINKS == group_q) & (sink_row < G * SINKS), s_s, LOW)
        top = jnp.maximum(jnp.max(s_d, axis=0, keepdims=True), jnp.max(s_s, axis=0, keepdims=True))
        p_d = jnp.exp2((s_d - top) * FACTOR)
        p_s = jnp.exp2((s_s - top) * FACTOR)
        den = jnp.sum(p_d, axis=0, keepdims=True) + jnp.sum(p_s, axis=0, keepdims=True)
        acc = dot(values(val_ref, at0), p_d.astype(jnp.bfloat16))
        acc = acc + dot(sink_v, p_s.astype(jnp.bfloat16))

        first = jnp.maximum(jnp.maximum(need[b] - base, b * QB - (W - 1)), 0) // CH
        n_suffix = b - first
        c0 = [jnp.minimum((need[(1 + g) * blocks + b] + 1) // CH, W // CH) for g in range(G)]
        n0, n1 = [W // CH - c for c in c0]
        total = n_suffix + n0 + n1

        def where_is(j):
            in0 = j - n_suffix
            in1 = in0 - n0
            at = jnp.where(
                in0 < 0,
                (first + j) * CH,
                jnp.where(
                    in1 < 0,
                    own + (c0[0] + in0) * CH,
                    jnp.where(j < total, own + W + (c0[1] + in1) * CH, 0),
                ),
            )
            kind = jnp.where(in0 < 0, 0, jnp.where(in1 < 0, 1, jnp.where(j < total, 2, 3)))
            return pl.multiple_of(at, CH), kind

        def low_of(kind):
            return low_ref[b, pl.ds(kind, 1), :]

        top, den, acc = visit(total, where_is, key_ref, val_ref, low_of, q_t, (top, den, acc))

        @pl.when(b < blocks // 2)
        def _():
            stat_ref[b, 0:1, :] = top
            stat_ref[b, 1:2, :] = den
            acc_ref[b] = acc

        @pl.when(b >= blocks // 2)
        def _():
            done = (acc / den).astype(jnp.bfloat16)
            upper_ref[2 * b - RING // 2] = done[:, 0:BLK]
            upper_ref[2 * b + 1 - RING // 2] = done[:, BLK:QB]

        return 0

    lax.fori_loop(0, blocks, one_block, 0)


def window_kernel(
    place, need, low_ref, query_ref, win_ref, upper_ref, stat_ref, acc_ref, out_ref,
    key_ref, val_ref,
):
    base = place[0] * RING * BLK
    blocks = RING * BLK // QB
    for j in range(RING // 2):
        key_ref[j * BLK : (j + 1) * BLK, :] = turn(win_ref[j, 0:HD, :])
        val_ref[j] = win_ref[j, HD : 2 * HD, :]
        out_ref[RING // 2 + j] = upper_ref[j]

    def one_block(b, _):
        q_t = query_block(query_ref, b)
        first = jnp.maximum(need[b] - base, b * QB - (W - 1)) + W
        first = jnp.minimum(first // CH, W // CH)
        total = W // CH - first

        def where_is(j):
            at = jnp.where(j < total, (first + j) * CH, 0)
            return pl.multiple_of(at, CH), jnp.where(j < total, 0, 1 + G)

        def low_of(kind):
            return low_ref[b, pl.ds(kind, 1), :] + jnp.where(kind == 0, W, 0)

        state = (stat_ref[b, 0:1, :], stat_ref[b, 1:2, :], acc_ref[b])
        _, den, acc = visit(total, where_is, key_ref, val_ref, low_of, q_t, state)
        done = (acc / den).astype(jnp.bfloat16)
        out_ref[2 * b] = done[:, 0:BLK]
        out_ref[2 * b + 1] = done[:, BLK:QB]
        return 0

    lax.fori_loop(0, blocks // 2, one_block, 0)


def project_kernel(side, attn_ref, w_ref, out_ref, half_ref, sum_ref, arrived):
    features = half_ref.shape[1]
    columns = pl.ds(pl.multiple_of(side[0] * features, features), features)
    parts = arrived.shape[0]
    tall = half_ref.shape[0] // parts
    loads = []
    for n in range(parts):
        rows = pl.ds(n * tall, tall)
        loads.append(
            pltpu.make_async_copy(w_ref.at[rows, columns], half_ref.at[rows, :], arrived.at[n])
        )
    for load in loads:
        load.start()
    turned = attn_ref[...].T
    for n in range(parts):
        loads[n].wait()
        at = slice(n * tall, (n + 1) * tall)
        part = dot(turned[:, at], half_ref[at, :])
        if n == 0:
            sum_ref[...] = part
        elif n < parts - 1:
            sum_ref[...] += part
        else:
            out_ref[...] = (sum_ref[...] + part).T.astype(out_ref.dtype)


def project(side, attn_t, w_out, dtype):
    width, rows = attn_t.shape
    features = w_out.shape[1] // 2
    return pl.pallas_call(
        project_kernel,
        out_shape=jax.ShapeDtypeStruct((features, rows), dtype),
        in_specs=[smem(), vmem(), pl.BlockSpec(memory_space=pltpu.HBM)],
        out_specs=vmem(),
        scratch_shapes=[
            pltpu.VMEM((width, features), jnp.bfloat16),
            pltpu.VMEM((rows, features), jnp.float32),
            pltpu.SemaphoreType.DMA((6,)),
        ],
        cost_estimate=pl.CostEstimate(
            flops=2 * width * features * rows,
            bytes_accessed=2 * width * features,
            transcendentals=0,
        ),
        compiler_params=pltpu.CompilerParams(vmem_limit_bytes=50 << 20),
        name="project",
    )(side.reshape(1), attn_t, w_out)


def vmem():
    return pl.BlockSpec(memory_space=pltpu.VMEM)


def smem():
    return pl.BlockSpec(memory_space=pltpu.SMEM)


def shards(
    queries, keys, values, cache_k, cache_v, sink_k, sink_v, suffix_lengths, request_group, w_out
):
    rows, width = queries.shape
    heads = width // HD
    seq = lax.axis_size("seq")
    rings = seq // RING
    device = lax.axis_index("seq")
    half = lax.axis_index("head")
    packed = pl.pallas_call(
        pack_kernel,
        out_shape=jax.ShapeDtypeStruct((heads, 2 * HD + 32, LANES), jnp.bfloat16),
        in_specs=[vmem()] * 4,
        out_specs=vmem(),
        name="pack",
    )(keys, values, cache_k, cache_v)
    packed_q, sinks = pl.pallas_call(
        pack_query_kernel,
        out_shape=(
            jax.ShapeDtypeStruct((heads, HD, LANES), jnp.bfloat16),
            jax.ShapeDtypeStruct((32, LANES), jnp.bfloat16),
        ),
        in_specs=[smem()] + [vmem()] * 3,
        out_specs=(vmem(), vmem()),
        cost_estimate=pl.CostEstimate(flops=1 << 20, bytes_accessed=1 << 21, transcendentals=0),
        name="pack_query",
    )((device % RING).reshape(1), queries, sink_k, sink_v)
    members = [[r * RING + i for i in range(RING)] for r in range(rings)]

    def trade(array, groups):
        return lax.all_to_all(array, "seq", 0, 0, axis_index_groups=groups, tiled=True)

    mine = trade(packed, members)
    mine_q = trade(packed_q, members)
    cache = mine[:, 2 * HD :, :]

    def send(array, dx, dy):
        pairs = []
        for r in range(rings):
            to = (r % 4 + dy) % 4 + 4 * ((r // 4 + dx) % 2)
            pairs += [(r * RING + i, to * RING + i) for i in range(RING)]
        return lax.ppermute(array, "seq", pairs)

    near_y = send(cache, 0, 3)
    near_x = send(cache, 1, 0)
    back_y = send(cache, 0, 1)
    far_y = send(near_y, 0, 3)
    near_xy = send(near_x, 0, 3)
    back_xy = send(back_y, 1, 0)
    far_xy = send(far_y, 1, 0)
    window = lax.ppermute(
        mine[RING // 2 :, : 2 * HD, :], "seq", [(s, s + RING) for s in range(seq - RING)]
    )
    caches = [cache, near_y, far_y, back_y, near_x, near_xy, far_xy, back_xy]
    own = RING * BLK
    blocks = own // QB
    place = (device // RING).reshape(1)
    turned, lows, need = pl.pallas_call(
        prep_kernel,
        out_shape=(
            jax.ShapeDtypeStruct((own, LANES), jnp.bfloat16),
            jax.ShapeDtypeStruct((blocks, 8, QB), jnp.int32),
            jax.ShapeDtypeStruct(((1 + G) * blocks,), jnp.int32),
        ),
        in_specs=[smem()] * 3 + [vmem()],
        out_specs=(vmem(), vmem(), smem()),
        cost_estimate=pl.CostEstimate(
            flops=1 << 20, bytes_accessed=1 << 22, transcendentals=0
        ),
        compiler_params=pltpu.CompilerParams(vmem_limit_bytes=VMEM_LIMIT),
        name="prep",
    )(place, suffix_lengths, request_group, mine)
    upper, stats, sums = pl.pallas_call(
        functools.partial(attend_kernel, rings=rings),
        out_shape=(
            jax.ShapeDtypeStruct((RING // 2, HD, BLK), jnp.bfloat16),
            jax.ShapeDtypeStruct((blocks // 2, 8, QB), jnp.float32),
            jax.ShapeDtypeStruct((blocks // 2, HD, QB), jnp.float32),
        ),
        in_specs=[smem()] * 2 + [vmem()] * (5 + rings),
        out_specs=(vmem(), vmem(), vmem()),
        scratch_shapes=[
            pltpu.VMEM((own + G * W, LANES), jnp.bfloat16),
            pltpu.VMEM(((own + G * W) // BLK, HD, BLK), jnp.bfloat16),
        ],
        cost_estimate=pl.CostEstimate(
            flops=own * 2 * W * HD * 4, bytes_accessed=1 << 22, transcendentals=own * 2 * W
        ),
        compiler_params=pltpu.CompilerParams(vmem_limit_bytes=VMEM_LIMIT),
        name="attend",
    )(place, need, lows, sinks, mine_q, mine, turned, *caches)
    attn = pl.pallas_call(
        window_kernel,
        out_shape=jax.ShapeDtypeStruct((RING, HD, BLK), jnp.bfloat16),
        in_specs=[smem()] * 2 + [vmem()] * 6,
        out_specs=vmem(),
        scratch_shapes=[
            pltpu.VMEM((W, LANES), jnp.bfloat16),
            pltpu.VMEM((W // BLK, HD, BLK), jnp.bfloat16),
        ],
        compiler_params=pltpu.CompilerParams(vmem_limit_bytes=VMEM_LIMIT),
        name="window",
    )(place, need, lows, mine_q, window, upper, stats, sums)
    attn_t = trade(attn, members).reshape(width, rows)
    give = project(1 - half, attn_t, w_out, jnp.bfloat16)
    got = lax.ppermute(give, "head", [(0, 1), (1, 0)])
    keep = project(half, attn_t, w_out, jnp.float32)
    return (keep + got.astype(jnp.float32)).astype(jnp.bfloat16)


def solution(mesh):
    placed = (
        P("seq", "head"),
        P("seq", "head"),
        P("seq", "head"),
        P("seq", "head"),
        P("seq", "head"),
        P(None, "head"),
        P(None, "head"),
        P(),
        P(),
        P("head", None),
    )
    return jax.shard_map(
        shards, mesh=mesh, in_specs=placed, out_specs=P("head", "seq"), check_vma=False
    )
```

```python
import functools
import math

import jax
import jax.numpy as jnp
from jax import lax
from jax.experimental import pallas as pl
from jax.experimental.pallas import tpu as pltpu
from jax.sharding import PartitionSpec as P

HD = 96
W = 1024
SINKS = 4
G = 2
RING = 16
BLK = 128
QB = 256
CH = 256
LANES = 128
FAR = 1 << 28
LOW = -1e30
VMEM_LIMIT = 24 << 20


def pack_kernel(k_ref, v_ref, ck_ref, cv_ref, out_ref):
    heads = k_ref.shape[1] // HD
    for which, ref in enumerate((k_ref, v_ref)):
        turned = ref[...].T
        for p in range(heads):
            out_ref[p, which * HD : (which + 1) * HD, :] = turned[p * HD : (p + 1) * HD, :]
    rows = ck_ref.shape[0]
    fill = jnp.zeros((rows, LANES - HD), ck_ref.dtype)
    for which, ref in enumerate((ck_ref, cv_ref)):
        for p in range(heads):
            piece = jnp.concatenate([ref[:, p * HD : (p + 1) * HD], fill], axis=1)
            base = 2 * HD + which * rows
            out_ref[p, base : base + rows, :] = piece


def gather_facts(place, lengths, groups, need, blocks):
    base = place[0] * RING * BLK
    own = RING * BLK
    for b in range((1 + G) * blocks):
        need[b] = FAR
    need[(1 + G) * blocks] = place[0]

    def one_request(r, carry):
        start, start_col, group_col = carry
        length = lengths[r]
        group = groups[r]
        first = jnp.where(start < base, 0, (start - base) // QB)
        last = jnp.minimum((start + length - 1 - base) // QB, blocks - 1)

        def mark(b, _):
            need[b] = jnp.minimum(need[b], start)
            offset = jnp.maximum(base + b * QB - start, 0)
            at = (1 + group) * blocks + b
            need[at] = jnp.minimum(need[at], offset)
            return 0

        @pl.when((start < base + own) & (start + length > base))
        def _():
            lax.fori_loop(first, last + 1, mark, 0)

        row = lax.broadcasted_iota(jnp.int32, start_col.shape, 0)
        start_col = jnp.where(row == r, start, start_col)
        group_col = jnp.where(row == r, group, group_col)
        return (start + length, start_col, group_col)

    reqs = lengths.shape[0]
    column = jnp.zeros((reqs, QB), jnp.int32)
    _, start_col, group_col = lax.fori_loop(0, reqs, one_request, (jnp.int32(0), column, column))
    return base, start_col, group_col


def query_facts(index, start_col, group_col):
    begun = start_col <= index
    start_q = jnp.max(jnp.where(begun, start_col, 0), axis=0, keepdims=True)
    here = begun & (start_col == start_q)
    group_q = jnp.max(jnp.where(here, group_col, 0), axis=0, keepdims=True)
    return jnp.maximum(start_q, index - (W - 1)), index - start_q, group_q


def turn(piece):
    pad = jnp.zeros((LANES - HD, BLK), jnp.bfloat16)
    return jnp.concatenate([piece, pad], axis=0).T


def query_block(query_ref, b):
    q_t = jnp.concatenate([query_ref[2 * b], query_ref[2 * b + 1]], axis=1)
    scaled = q_t.astype(jnp.float32) * FACTOR
    high = scaled.astype(jnp.bfloat16)
    low = (scaled - high.astype(jnp.float32)).astype(jnp.bfloat16)
    pad = jnp.zeros((LANES - HD, QB), jnp.bfloat16)
    return jnp.concatenate([high, pad, low, pad], axis=0)


def score(keys, q_t):
    return dot(jnp.concatenate([keys, keys], axis=1), q_t)


def values(val_ref, at):
    slot = at // BLK
    return jnp.concatenate([val_ref[slot], val_ref[slot + 1]], axis=1)


def dot(a, b):
    return jnp.dot(a, b, preferred_element_type=jnp.float32)


FACTOR = (1.0 / math.sqrt(HD)) * math.log2(math.e)


def prep_kernel(
    need_in, sink_in, low_in, own_ref, key_ref, need, sink_ref, low_ref, last_ref
):
    for j in range(RING // 2):
        last_ref[j] = own_ref[RING // 2 + j, 0 : 2 * HD, :]
    sink_ref[...] = sink_in[...]
    low_ref[...] = low_in[...]
    for n in range(need.shape[0]):
        need[n] = need_in[n]
    for j in range(RING):
        key_ref[j * BLK : (j + 1) * BLK, :] = turn(own_ref[j, 0:HD, :])


def pack_query_kernel(
    place, lengths, groups, q_ref, sk_ref, sv_ref, query_ref, sink_ref, low_ref, need
):
    turned = q_ref[...].T
    for p in range(q_ref.shape[1] // HD):
        query_ref[p] = turned[p * HD : (p + 1) * HD, :]
    width = sk_ref.shape[1]
    column = lax.broadcasted_iota(jnp.int32, (width, LANES), 0)
    lane = lax.broadcasted_iota(jnp.int32, (width, LANES), 1)
    pick = ((column == place[1] * HD + lane) & (lane < HD)).astype(jnp.float32).astype(jnp.bfloat16)
    for which, ref in enumerate((sk_ref, sv_ref)):
        piece = jnp.dot(ref[...], pick, preferred_element_type=jnp.float32)
        piece = jnp.concatenate([piece, jnp.zeros_like(piece)], axis=0)
        sink_ref[which * 16 : (which + 1) * 16, :] = piece.astype(jnp.bfloat16)
    own = RING * BLK
    blocks = own // QB
    cache_at = own
    base, start_col, group_col = gather_facts(place, lengths, groups, need, blocks)
    lane = lax.broadcasted_iota(jnp.int32, (1, QB), 1)
    for b in range(blocks):
        index = base + b * QB + lane
        low_q, offset, group_q = query_facts(index, start_col, group_col)
        low_ref[b, 0:1, :] = low_q - base
        for g in range(G):
            low_ref[b, 1 + g : 2 + g, :] = jnp.where(
                group_q == g, cache_at + g * W + offset + 1, FAR
            )
        low_ref[b, 1 + G : 2 + G, :] = jnp.full((1, QB), FAR, jnp.int32)
        low_ref[b, 2 + G : 3 + G, :] = group_q


def fold(rows, how):
    return how(rows.reshape(rows.shape[0] // 8, 8, QB), axis=0)


def visit(total, where_is, key_ref, val_ref, low_of, q_t, state):
    row_iota = lax.broadcasted_iota(jnp.int32, (CH, QB), 0)

    def step(j, state):
        top, den, acc = state
        scores, ats = [], []
        for u in range(2):
            at, kind = where_is(2 * j + u)
            s = score(key_ref[pl.ds(at, CH), :], q_t)
            scores.append(jnp.where(row_iota >= low_of(kind) - at, s, LOW))
            ats.append(at)
        peak = jnp.maximum(fold(scores[0], jnp.max), fold(scores[1], jnp.max))
        new = jnp.maximum(top, jnp.max(peak, axis=0, keepdims=True))
        fade = jnp.exp2(top - new)
        den = den * fade
        ps = []
        for u in range(2):
            p = jnp.exp2(scores[u] - new)
            den = den + fold(p, jnp.sum)
            ps.append(p.astype(jnp.bfloat16))
        vals = jnp.concatenate([values(val_ref, at) for at in ats], axis=1)
        acc = acc * fade + dot(vals, jnp.concatenate(ps, axis=0))
        return (new, den, acc)

    return lax.fori_loop(0, (total + 1) // 2, step, state)


def attend_kernel(
    need, low_ref, sink_ref, query_ref, own_ref, turned_ref, *rest, rings
):
    caches = rest[:rings]
    upper_ref, stat_ref, acc_ref, key_ref, val_ref = rest[rings:]
    own = RING * BLK
    blocks = own // QB
    ring = need[(1 + G) * blocks]
    base = ring * own
    key_ref[0:own, :] = turned_ref[...]
    for j in range(RING):
        val_ref[j] = own_ref[j, HD : 2 * HD, :]
    rows = RING * 16
    for k in range(rings):
        source = lax.rem(lax.rem(ring, 4) + k % 4, 4) + 4 * lax.rem(ring // 4 + k // 4, 2)
        piece = caches[k][...]
        at = pl.multiple_of(own + source * rows, rows)
        key_ref[pl.ds(at, rows), :] = piece[:, 0:16, :].reshape(rows, LANES)
        turned = piece[:, 16:32, :].reshape(rows, LANES).T
        for half in range(rows // BLK):
            val_ref[at // BLK + half] = turned[0:HD, half * BLK : (half + 1) * BLK]
    lane = lax.broadcasted_iota(jnp.int32, (1, QB), 1)
    row_iota = lax.broadcasted_iota(jnp.int32, (CH, QB), 0)
    sink_row = lax.broadcasted_iota(jnp.int32, (16, QB), 0)
    sink_v = sink_ref[16:32, :].T[0:HD, :]

    def one_block(b, _):
        low_suffix = low_ref[b, 0:1, :]
        group_q = low_ref[b, 2 + G : 3 + G, :]
        q_t = query_block(query_ref, b)
        at0 = pl.multiple_of(b * QB, CH)
        s_d = score(key_ref[pl.ds(at0, CH), :], q_t)
        s_d = jnp.where((row_iota >= low_suffix - at0) & (row_iota <= lane), s_d, LOW)
        s_s = score(sink_ref[0:16, :], q_t)
        s_s = jnp.where((sink_row // SINKS == group_q) & (sink_row < G * SINKS), s_s, LOW)
        top = jnp.maximum(jnp.max(s_d, axis=0, keepdims=True), jnp.max(s_s, axis=0, keepdims=True))
        p_d = jnp.exp2(s_d - top)
        p_s = jnp.exp2(s_s - top)
        den = fold(p_d, jnp.sum) + fold(p_s, jnp.sum)
        acc = dot(values(val_ref, at0), p_d.astype(jnp.bfloat16))
        acc = acc + dot(sink_v, p_s.astype(jnp.bfloat16))

        first = jnp.maximum(jnp.maximum(need[b] - base, b * QB - (W - 1)), 0) // CH
        n_suffix = b - first
        c0 = [jnp.minimum((need[(1 + g) * blocks + b] + 1) // CH, W // CH) for g in range(G)]
        n0, n1 = [W // CH - c for c in c0]
        total = n_suffix + n0 + n1

        def where_is(j):
            in0 = j - n_suffix
            in1 = in0 - n0
            at = jnp.where(
                in0 < 0,
                (first + j) * CH,
                jnp.where(
                    in1 < 0,
                    own + (c0[0] + in0) * CH,
                    jnp.where(j < total, own + W + (c0[1] + in1) * CH, 0),
                ),
            )
            kind = jnp.where(in0 < 0, 0, jnp.where(in1 < 0, 1, jnp.where(j < total, 2, 3)))
            return pl.multiple_of(at, CH), kind

        def low_of(kind):
            return low_ref[b, pl.ds(kind, 1), :]

        state = (top, den, acc)
        top, den, acc = visit(total, where_is, key_ref, val_ref, low_of, q_t, state)

        @pl.when(b < blocks // 2)
        def _():
            stat_ref[b, 0:8, :] = jnp.broadcast_to(top, (8, QB))
            stat_ref[b, 8:16, :] = den
            acc_ref[b] = acc

        @pl.when(b >= blocks // 2)
        def _():
            done = (acc / jnp.sum(den, axis=0, keepdims=True)).astype(jnp.bfloat16)
            upper_ref[2 * b - RING // 2] = done[:, 0:BLK]
            upper_ref[2 * b + 1 - RING // 2] = done[:, BLK:QB]

        return 0

    lax.fori_loop(0, blocks, one_block, 0)


def window_kernel(
    need, low_ref, query_ref, win_ref, upper_ref, stat_ref, acc_ref, out_ref,
    key_ref, val_ref,
):
    blocks = RING * BLK // QB
    base = need[(1 + G) * blocks] * RING * BLK
    for j in range(RING // 2):
        key_ref[j * BLK : (j + 1) * BLK, :] = turn(win_ref[j, 0:HD, :])
        val_ref[j] = win_ref[j, HD : 2 * HD, :]
        out_ref[RING // 2 + j] = upper_ref[j]

    def one_block(b, _):
        q_t = query_block(query_ref, b)
        first = jnp.maximum(need[b] - base, b * QB - (W - 1)) + W
        first = jnp.minimum(first // CH, W // CH)
        total = W // CH - first

        def where_is(j):
            at = jnp.where(j < total, (first + j) * CH, 0)
            return pl.multiple_of(at, CH), jnp.where(j < total, 0, 1 + G)

        def low_of(kind):
            return low_ref[b, pl.ds(kind, 1), :] + jnp.where(kind == 0, W, 0)

        state = (stat_ref[b, 0:1, :], stat_ref[b, 8:16, :], acc_ref[b])
        _, den, acc = visit(total, where_is, key_ref, val_ref, low_of, q_t, state)
        done = (acc / jnp.sum(den, axis=0, keepdims=True)).astype(jnp.bfloat16)
        out_ref[2 * b] = done[:, 0:BLK]
        out_ref[2 * b + 1] = done[:, BLK:QB]
        return 0

    lax.fori_loop(0, blocks // 2, one_block, 0)


def project_kernel(side, attn_ref, w_ref, out_ref, half_ref, sum_ref, arrived):
    features = half_ref.shape[1]
    columns = pl.ds(pl.multiple_of(side[0] * features, features), features)
    parts = arrived.shape[0]
    tall = half_ref.shape[0] // parts
    loads = []
    for n in range(parts):
        rows = pl.ds(n * tall, tall)
        loads.append(
            pltpu.make_async_copy(w_ref.at[rows, columns], half_ref.at[rows, :], arrived.at[n])
        )
    for load in loads:
        load.start()
    turned = attn_ref[...].T
    for n in range(parts):
        loads[n].wait()
        at = slice(n * tall, (n + 1) * tall)
        part = dot(turned[:, at], half_ref[at, :])
        if n == 0:
            sum_ref[...] = part
        elif n < parts - 1:
            sum_ref[...] += part
        else:
            out_ref[...] = (sum_ref[...] + part).T.astype(out_ref.dtype)


def project(side, attn_t, w_out, dtype):
    width, rows = attn_t.shape
    features = w_out.shape[1] // 2
    return pl.pallas_call(
        project_kernel,
        out_shape=jax.ShapeDtypeStruct((features, rows), dtype),
        in_specs=[smem(), vmem(), pl.BlockSpec(memory_space=pltpu.HBM)],
        out_specs=vmem(),
        scratch_shapes=[
            pltpu.VMEM((width, features), jnp.bfloat16),
            pltpu.VMEM((rows, features), jnp.float32),
            pltpu.SemaphoreType.DMA((6,)),
        ],
        cost_estimate=pl.CostEstimate(
            flops=2 * width * features * rows,
            bytes_accessed=2 * width * features,
            transcendentals=0,
        ),
        compiler_params=pltpu.CompilerParams(vmem_limit_bytes=50 << 20),
        name="project",
    )(side.reshape(1), attn_t, w_out)


def vmem():
    return pl.BlockSpec(memory_space=pltpu.VMEM)


def smem():
    return pl.BlockSpec(memory_space=pltpu.SMEM)


def shards(
    queries, keys, values, cache_k, cache_v, sink_k, sink_v, suffix_lengths, request_group, w_out
):
    rows, width = queries.shape
    heads = width // HD
    seq = lax.axis_size("seq")
    rings = seq // RING
    device = lax.axis_index("seq")
    half = lax.axis_index("head")
    packed = pl.pallas_call(
        pack_kernel,
        out_shape=jax.ShapeDtypeStruct((heads, 2 * HD + 32, LANES), jnp.bfloat16),
        in_specs=[vmem()] * 4,
        out_specs=vmem(),
        name="pack",
    )(keys, values, cache_k, cache_v)
    own = RING * BLK
    blocks = own // QB
    place = jnp.stack([device // RING, device % RING]).astype(jnp.int32)
    packed_q, sinks, lows, need = pl.pallas_call(
        pack_query_kernel,
        out_shape=(
            jax.ShapeDtypeStruct((heads, HD, LANES), jnp.bfloat16),
            jax.ShapeDtypeStruct((32, LANES), jnp.bfloat16),
            jax.ShapeDtypeStruct((blocks, 8, QB), jnp.int32),
            jax.ShapeDtypeStruct(((1 + G) * blocks + 1,), jnp.int32),
        ),
        in_specs=[smem()] * 3 + [vmem()] * 3,
        out_specs=(vmem(), vmem(), vmem(), smem()),
        cost_estimate=pl.CostEstimate(flops=1 << 20, bytes_accessed=1 << 21, transcendentals=0),
        name="pack_query",
    )(place, suffix_lengths, request_group, queries, sink_k, sink_v)
    members = [[r * RING + i for i in range(RING)] for r in range(rings)]

    def trade(array, groups):
        return lax.all_to_all(array, "seq", 0, 0, axis_index_groups=groups, tiled=True)

    mine = trade(packed, members)
    mine_q = trade(packed_q, members)
    cache = mine[:, 2 * HD :, :]

    def send(array, dx, dy):
        pairs = []
        for r in range(rings):
            to = (r % 4 + dy) % 4 + 4 * ((r // 4 + dx) % 2)
            pairs += [(r * RING + i, to * RING + i) for i in range(RING)]
        return lax.ppermute(array, "seq", pairs)

    near_y = send(cache, 0, 3)
    near_x = send(cache, 1, 0)
    back_y = send(cache, 0, 1)
    far_y = send(cache, 0, 2)
    near_xy = send(near_x, 0, 3)
    back_xy = send(back_y, 1, 0)
    far_xy = send(far_y, 1, 0)
    caches = [cache, near_y, far_y, back_y, near_x, near_xy, far_xy, back_xy]
    turned, need, sinks, lows, last = pl.pallas_call(
        prep_kernel,
        out_shape=(
            jax.ShapeDtypeStruct((own, LANES), jnp.bfloat16),
            jax.ShapeDtypeStruct(need.shape, need.dtype),
            jax.ShapeDtypeStruct(sinks.shape, sinks.dtype),
            jax.ShapeDtypeStruct(lows.shape, lows.dtype),
            jax.ShapeDtypeStruct((RING // 2, 2 * HD, LANES), jnp.bfloat16),
        ),
        in_specs=[smem()] + [vmem()] * 3,
        out_specs=(vmem(), smem(), vmem(), vmem(), vmem()),
        cost_estimate=pl.CostEstimate(
            flops=1 << 20, bytes_accessed=1 << 22, transcendentals=0
        ),
        compiler_params=pltpu.CompilerParams(vmem_limit_bytes=VMEM_LIMIT),
        name="prep",
    )(need, sinks, lows, mine)
    window = lax.ppermute(last, "seq", [(s, s + RING) for s in range(seq - RING)])
    upper, stats, sums = pl.pallas_call(
        functools.partial(attend_kernel, rings=rings),
        out_shape=(
            jax.ShapeDtypeStruct((RING // 2, HD, BLK), jnp.bfloat16),
            jax.ShapeDtypeStruct((blocks // 2, 16, QB), jnp.float32),
            jax.ShapeDtypeStruct((blocks // 2, HD, QB), jnp.float32),
        ),
        in_specs=[smem()] + [vmem()] * (5 + rings),
        out_specs=(vmem(), vmem(), vmem()),
        scratch_shapes=[
            pltpu.VMEM((own + G * W, LANES), jnp.bfloat16),
            pltpu.VMEM(((own + G * W) // BLK, HD, BLK), jnp.bfloat16),
        ],
        cost_estimate=pl.CostEstimate(
            flops=own * 2 * W * HD * 4, bytes_accessed=1 << 22, transcendentals=own * 2 * W
        ),
        compiler_params=pltpu.CompilerParams(vmem_limit_bytes=VMEM_LIMIT),
        name="attend",
    )(need, lows, sinks, mine_q, mine, turned, *caches)
    attn = pl.pallas_call(
        window_kernel,
        out_shape=jax.ShapeDtypeStruct((RING, HD, BLK), jnp.bfloat16),
        in_specs=[smem()] + [vmem()] * 6,
        out_specs=vmem(),
        scratch_shapes=[
            pltpu.VMEM((W, LANES), jnp.bfloat16),
            pltpu.VMEM((W // BLK, HD, BLK), jnp.bfloat16),
        ],
        compiler_params=pltpu.CompilerParams(vmem_limit_bytes=VMEM_LIMIT),
        name="window",
    )(need, lows, mine_q, window, upper, stats, sums)
    attn_t = trade(attn, members).reshape(width, rows)
    give = project(1 - half, attn_t, w_out, jnp.bfloat16)
    got = lax.ppermute(give, "head", [(0, 1), (1, 0)])
    keep = project(half, attn_t, w_out, jnp.float32)
    return (keep + got.astype(jnp.float32)).astype(jnp.bfloat16)


def solution(mesh):
    placed = (
        P("seq", "head"),
        P("seq", "head"),
        P("seq", "head"),
        P("seq", "head"),
        P("seq", "head"),
        P(None, "head"),
        P(None, "head"),
        P(),
        P(),
        P("head", None),
    )
    return jax.shard_map(
        shards, mesh=mesh, in_specs=placed, out_specs=P("head", "seq"), check_vma=False
    )
```

```python
import functools
import math

import jax
import jax.numpy as jnp
from jax import lax
from jax.experimental import pallas as pl
from jax.experimental.pallas import tpu as pltpu
from jax.sharding import PartitionSpec as P

HD = 96
W = 1024
SINKS = 4
G = 2
RING = 16
BLK = 128
QB = 256
CH = 256
LANES = 128
FAR = 1 << 28
LOW = -1e30
VMEM_LIMIT = 24 << 20
PIECE = 256


def pack_kernel(k_ref, v_ref, ck_ref, cv_ref, out_ref):
    heads = k_ref.shape[1] // HD
    for which, ref in enumerate((k_ref, v_ref)):
        turned = ref[...].T
        for p in range(heads):
            out_ref[p, which * HD : (which + 1) * HD, :] = turned[p * HD : (p + 1) * HD, :]
    rows = ck_ref.shape[0]
    fill = jnp.zeros((rows, LANES - HD), ck_ref.dtype)
    for which, ref in enumerate((ck_ref, cv_ref)):
        for p in range(heads):
            piece = jnp.concatenate([ref[:, p * HD : (p + 1) * HD], fill], axis=1)
            base = 2 * HD + which * rows
            out_ref[p, base : base + rows, :] = piece


def gather_facts(place, lengths, groups, need, blocks):
    base = place[0] * RING * BLK
    own = RING * BLK
    for b in range((1 + G) * blocks):
        need[b] = FAR
    need[(1 + G) * blocks] = place[0]

    def one_request(r, carry):
        start, start_col, group_col = carry
        length = lengths[r]
        group = groups[r]
        first = jnp.where(start < base, 0, (start - base) // QB)
        last = jnp.minimum((start + length - 1 - base) // QB, blocks - 1)

        def mark(b, _):
            need[b] = jnp.minimum(need[b], start)
            offset = jnp.maximum(base + b * QB - start, 0)
            at = (1 + group) * blocks + b
            need[at] = jnp.minimum(need[at], offset)
            return 0

        @pl.when((start < base + own) & (start + length > base))
        def _():
            lax.fori_loop(first, last + 1, mark, 0)

        row = lax.broadcasted_iota(jnp.int32, start_col.shape, 0)
        start_col = jnp.where(row == r, start, start_col)
        group_col = jnp.where(row == r, group, group_col)
        return (start + length, start_col, group_col)

    reqs = lengths.shape[0]
    column = jnp.zeros((reqs, QB), jnp.int32)
    _, start_col, group_col = lax.fori_loop(0, reqs, one_request, (jnp.int32(0), column, column))
    return base, start_col, group_col


def query_facts(index, start_col, group_col):
    begun = start_col <= index
    start_q = jnp.max(jnp.where(begun, start_col, 0), axis=0, keepdims=True)
    here = begun & (start_col == start_q)
    group_q = jnp.max(jnp.where(here, group_col, 0), axis=0, keepdims=True)
    return jnp.maximum(start_q, index - (W - 1)), index - start_q, group_q


def turn(piece):
    pad = jnp.zeros((LANES - HD, BLK), jnp.bfloat16)
    return jnp.concatenate([piece, pad], axis=0).T


def query_block(query_ref, b):
    q_t = jnp.concatenate([query_ref[2 * b], query_ref[2 * b + 1]], axis=1)
    return jnp.concatenate([q_t, jnp.zeros((LANES - HD, QB), jnp.bfloat16)], axis=0)


def values(val_ref, at):
    slot = at // BLK
    return jnp.concatenate([val_ref[slot], val_ref[slot + 1]], axis=1)


def dot(a, b):
    return jnp.dot(a, b, preferred_element_type=jnp.float32)


FACTOR = (1.0 / math.sqrt(HD)) * math.log2(math.e)


def prep_kernel(own_ref, key_ref, last_ref):
    for j in range(RING // 2):
        last_ref[j] = own_ref[RING // 2 + j, 0 : 2 * HD, :]
    for j in range(RING):
        key_ref[j * BLK : (j + 1) * BLK, :] = turn(own_ref[j, 0:HD, :])


def pack_query_kernel(
    place, lengths, groups, q_ref, sk_ref, sv_ref, query_ref, sink_ref, low_ref, need
):
    turned = q_ref[...].T
    for p in range(q_ref.shape[1] // HD):
        query_ref[p] = turned[p * HD : (p + 1) * HD, :]
    width = sk_ref.shape[1]
    column = lax.broadcasted_iota(jnp.int32, (width, LANES), 0)
    lane = lax.broadcasted_iota(jnp.int32, (width, LANES), 1)
    pick = ((column == place[1] * HD + lane) & (lane < HD)).astype(jnp.float32).astype(jnp.bfloat16)
    for which, ref in enumerate((sk_ref, sv_ref)):
        piece = jnp.dot(ref[...], pick, preferred_element_type=jnp.float32)
        piece = jnp.concatenate([piece, jnp.zeros_like(piece)], axis=0)
        sink_ref[which * 16 : (which + 1) * 16, :] = piece.astype(jnp.bfloat16)
    own = RING * BLK
    blocks = own // QB
    cache_at = own
    base, start_col, group_col = gather_facts(place, lengths, groups, need, blocks)
    lane = lax.broadcasted_iota(jnp.int32, (1, QB), 1)
    for b in range(blocks):
        index = base + b * QB + lane
        low_q, offset, group_q = query_facts(index, start_col, group_col)
        low_ref[b, 0:1, :] = low_q - base
        for g in range(G):
            low_ref[b, 1 + g : 2 + g, :] = jnp.where(
                group_q == g, cache_at + g * W + offset + 1, FAR
            )
        low_ref[b, 1 + G : 2 + G, :] = jnp.full((1, QB), FAR, jnp.int32)
        low_ref[b, 2 + G : 3 + G, :] = group_q


def fold(rows, how):
    return how(rows.reshape(rows.shape[0] // 8, 8, QB), axis=0)


def visit(total, where_is, key_ref, val_ref, low_of, q_t, state, buffers):
    s_even, s_odd, p_even, p_odd = buffers
    row_iota = lax.broadcasted_iota(jnp.int32, (PIECE, QB), 0)
    pieces = [slice(n * PIECE, (n + 1) * PIECE) for n in range(CH // PIECE)]

    def scores(j, ref):
        at, kind = where_is(j)
        low = low_of(kind) - at
        peak = None
        for n, rows in enumerate(pieces):
            s = dot(key_ref[pl.ds(at + n * PIECE, PIECE), :], q_t)
            s = jnp.where(row_iota >= low - n * PIECE, s, LOW)
            ref[rows, :] = s
            high = fold(s, jnp.max)
            peak = high if peak is None else jnp.maximum(peak, high)
        return peak, at

    def weigh(s_ref, p_ref, peak, top, den):
        new = jnp.maximum(top, jnp.max(peak, axis=0, keepdims=True))
        fade = jnp.exp2((top - new) * FACTOR)
        den = den * fade
        for rows in pieces:
            p = jnp.exp2((s_ref[rows, :] - new) * FACTOR)
            den = den + fold(p, jnp.sum)
            p_ref[rows, :] = p.astype(jnp.bfloat16)
        return new, fade, den

    top, den, acc, before = state
    peak, at = scores(0, s_even)

    def step(j, state):
        top, den, acc, before, peak, at = state
        next_peak, next_at = scores(2 * j + 1, s_odd)
        acc = acc + dot(values(val_ref, before), p_odd[...])
        top, fade, den = weigh(s_even, p_even, peak, top, den)
        acc = acc * fade + dot(values(val_ref, at), p_even[...])
        peak, last_at = scores(2 * j + 2, s_even)
        top, fade, den = weigh(s_odd, p_odd, next_peak, top, den)
        acc = acc * fade
        return (top, den, acc, next_at, peak, last_at)

    top, den, acc, before, _, _ = lax.fori_loop(
        0, (total + 1) // 2, step, (top, den, acc, before, peak, at)
    )
    return top, den, acc + dot(values(val_ref, before), p_odd[...])


def attend_kernel(
    need, low_ref, sink_ref, query_ref, own_ref, turned_ref, *rest, rings
):
    caches = rest[:rings]
    upper_ref, stat_ref, acc_ref, key_ref, val_ref = rest[rings : rings + 5]
    buffers = rest[rings + 5 :]
    own = RING * BLK
    blocks = own // QB
    ring = need[(1 + G) * blocks]
    base = ring * own
    key_ref[0:own, :] = turned_ref[...]
    for j in range(RING):
        val_ref[j] = own_ref[j, HD : 2 * HD, :]
    rows = RING * 16
    for k in range(rings):
        source = lax.rem(lax.rem(ring, 4) + k % 4, 4) + 4 * lax.rem(ring // 4 + k // 4, 2)
        piece = caches[k][...]
        at = pl.multiple_of(own + source * rows, rows)
        key_ref[pl.ds(at, rows), :] = piece[:, 0:16, :].reshape(rows, LANES)
        turned = piece[:, 16:32, :].reshape(rows, LANES).T
        for half in range(rows // BLK):
            val_ref[at // BLK + half] = turned[0:HD, half * BLK : (half + 1) * BLK]
    lane = lax.broadcasted_iota(jnp.int32, (1, QB), 1)
    row_iota = lax.broadcasted_iota(jnp.int32, (CH, QB), 0)
    sink_row = lax.broadcasted_iota(jnp.int32, (16, QB), 0)
    sink_v = sink_ref[16:32, :].T[0:HD, :]

    def one_block(b, _):
        low_suffix = low_ref[b, 0:1, :]
        group_q = low_ref[b, 2 + G : 3 + G, :]
        q_t = query_block(query_ref, b)
        at0 = pl.multiple_of(b * QB, CH)
        s_d = dot(key_ref[pl.ds(at0, CH), :], q_t)
        s_d = jnp.where((row_iota >= low_suffix - at0) & (row_iota <= lane), s_d, LOW)
        s_s = dot(sink_ref[0:16, :], q_t)
        s_s = jnp.where((sink_row // SINKS == group_q) & (sink_row < G * SINKS), s_s, LOW)
        top = jnp.maximum(jnp.max(s_d, axis=0, keepdims=True), jnp.max(s_s, axis=0, keepdims=True))
        p_d = jnp.exp2((s_d - top) * FACTOR)
        p_s = jnp.exp2((s_s - top) * FACTOR)
        den = fold(p_d, jnp.sum) + fold(p_s, jnp.sum)
        buffers[3][...] = p_d.astype(jnp.bfloat16)
        acc = dot(sink_v, p_s.astype(jnp.bfloat16))

        first = jnp.maximum(jnp.maximum(need[b] - base, b * QB - (W - 1)), 0) // CH
        n_suffix = b - first
        c0 = [jnp.minimum((need[(1 + g) * blocks + b] + 1) // CH, W // CH) for g in range(G)]
        n0, n1 = [W // CH - c for c in c0]
        total = n_suffix + n0 + n1

        def where_is(j):
            in0 = j - n_suffix
            in1 = in0 - n0
            at = jnp.where(
                in0 < 0,
                (first + j) * CH,
                jnp.where(
                    in1 < 0,
                    own + (c0[0] + in0) * CH,
                    jnp.where(j < total, own + W + (c0[1] + in1) * CH, 0),
                ),
            )
            kind = jnp.where(in0 < 0, 0, jnp.where(in1 < 0, 1, jnp.where(j < total, 2, 3)))
            return pl.multiple_of(at, CH), kind

        def low_of(kind):
            return low_ref[b, pl.ds(kind, 1), :]

        state = (top, den, acc, at0)
        top, den, acc = visit(total, where_is, key_ref, val_ref, low_of, q_t, state, buffers)

        @pl.when(b < blocks // 2)
        def _():
            stat_ref[b, 0:8, :] = jnp.broadcast_to(top, (8, QB))
            stat_ref[b, 8:16, :] = den
            acc_ref[b] = acc

        @pl.when(b >= blocks // 2)
        def _():
            done = (acc / jnp.sum(den, axis=0, keepdims=True)).astype(jnp.bfloat16)
            upper_ref[2 * b - RING // 2] = done[:, 0:BLK]
            upper_ref[2 * b + 1 - RING // 2] = done[:, BLK:QB]

        return 0

    lax.fori_loop(0, blocks, one_block, 0)


def window_kernel(
    need, low_ref, query_ref, win_ref, upper_ref, stat_ref, acc_ref, out_ref,
    key_ref, val_ref, *buffers,
):
    blocks = RING * BLK // QB
    base = need[(1 + G) * blocks] * RING * BLK
    for j in range(RING // 2):
        key_ref[j * BLK : (j + 1) * BLK, :] = turn(win_ref[j, 0:HD, :])
        val_ref[j] = win_ref[j, HD : 2 * HD, :]
        out_ref[RING // 2 + j] = upper_ref[j]

    def one_block(b, _):
        q_t = query_block(query_ref, b)
        first = jnp.maximum(need[b] - base, b * QB - (W - 1)) + W
        first = jnp.minimum(first // CH, W // CH)
        total = W // CH - first

        def where_is(j):
            at = jnp.where(j < total, (first + j) * CH, 0)
            return pl.multiple_of(at, CH), jnp.where(j < total, 0, 1 + G)

        def low_of(kind):
            return low_ref[b, pl.ds(kind, 1), :] + jnp.where(kind == 0, W, 0)

        buffers[3][...] = jnp.zeros((CH, QB), jnp.bfloat16)
        state = (stat_ref[b, 0:1, :], stat_ref[b, 8:16, :], acc_ref[b], jnp.int32(0))
        _, den, acc = visit(total, where_is, key_ref, val_ref, low_of, q_t, state, buffers)
        done = (acc / jnp.sum(den, axis=0, keepdims=True)).astype(jnp.bfloat16)
        out_ref[2 * b] = done[:, 0:BLK]
        out_ref[2 * b + 1] = done[:, BLK:QB]
        return 0

    lax.fori_loop(0, blocks // 2, one_block, 0)


def project_kernel(side, attn_ref, w_ref, out_ref, half_ref, sum_ref, arrived):
    features = half_ref.shape[1]
    columns = pl.ds(pl.multiple_of(side[0] * features, features), features)
    parts = arrived.shape[0]
    tall = half_ref.shape[0] // parts
    loads = []
    for n in range(parts):
        rows = pl.ds(n * tall, tall)
        loads.append(
            pltpu.make_async_copy(w_ref.at[rows, columns], half_ref.at[rows, :], arrived.at[n])
        )
    for load in loads:
        load.start()
    turned = attn_ref[...].T
    for n in range(parts):
        loads[n].wait()
        at = slice(n * tall, (n + 1) * tall)
        part = dot(turned[:, at], half_ref[at, :])
        if n == 0:
            sum_ref[...] = part
        elif n < parts - 1:
            sum_ref[...] += part
        else:
            out_ref[...] = (sum_ref[...] + part).T.astype(out_ref.dtype)


def project(side, attn_t, w_out, dtype):
    width, rows = attn_t.shape
    features = w_out.shape[1] // 2
    return pl.pallas_call(
        project_kernel,
        out_shape=jax.ShapeDtypeStruct((features, rows), dtype),
        in_specs=[smem(), vmem(), pl.BlockSpec(memory_space=pltpu.HBM)],
        out_specs=vmem(),
        scratch_shapes=[
            pltpu.VMEM((width, features), jnp.bfloat16),
            pltpu.VMEM((rows, features), jnp.float32),
            pltpu.SemaphoreType.DMA((6,)),
        ],
        cost_estimate=pl.CostEstimate(
            flops=2 * width * features * rows,
            bytes_accessed=2 * width * features,
            transcendentals=0,
        ),
        compiler_params=pltpu.CompilerParams(vmem_limit_bytes=50 << 20),
        name="project",
    )(side.reshape(1), attn_t, w_out)


def vmem():
    return pl.BlockSpec(memory_space=pltpu.VMEM)


def smem():
    return pl.BlockSpec(memory_space=pltpu.SMEM)


def shards(
    queries, keys, values, cache_k, cache_v, sink_k, sink_v, suffix_lengths, request_group, w_out
):
    rows, width = queries.shape
    heads = width // HD
    seq = lax.axis_size("seq")
    rings = seq // RING
    device = lax.axis_index("seq")
    half = lax.axis_index("head")
    packed = pl.pallas_call(
        pack_kernel,
        out_shape=jax.ShapeDtypeStruct((heads, 2 * HD + 32, LANES), jnp.bfloat16),
        in_specs=[vmem()] * 4,
        out_specs=vmem(),
        name="pack",
    )(keys, values, cache_k, cache_v)
    own = RING * BLK
    blocks = own // QB
    place = jnp.stack([device // RING, device % RING]).astype(jnp.int32)
    packed_q, sinks, lows, need = pl.pallas_call(
        pack_query_kernel,
        out_shape=(
            jax.ShapeDtypeStruct((heads, HD, LANES), jnp.bfloat16),
            jax.ShapeDtypeStruct((32, LANES), jnp.bfloat16),
            jax.ShapeDtypeStruct((blocks, 8, QB), jnp.int32),
            jax.ShapeDtypeStruct(((1 + G) * blocks + 1,), jnp.int32),
        ),
        in_specs=[smem()] * 3 + [vmem()] * 3,
        out_specs=(vmem(), vmem(), vmem(), smem()),
        cost_estimate=pl.CostEstimate(flops=1 << 20, bytes_accessed=1 << 21, transcendentals=0),
        compiler_params=pltpu.CompilerParams(vmem_limit_bytes=VMEM_LIMIT),
        name="pack_query",
    )(place, suffix_lengths, request_group, queries, sink_k, sink_v)
    members = [[r * RING + i for i in range(RING)] for r in range(rings)]

    def trade(array, groups):
        return lax.all_to_all(array, "seq", 0, 0, axis_index_groups=groups, tiled=True)

    mine = trade(packed, members)
    mine_q = trade(packed_q, members)
    cache = mine[:, 2 * HD :, :]

    def send(array, dx, dy):
        pairs = []
        for r in range(rings):
            to = (r % 4 + dy) % 4 + 4 * ((r // 4 + dx) % 2)
            pairs += [(r * RING + i, to * RING + i) for i in range(RING)]
        return lax.ppermute(array, "seq", pairs)

    near_y = send(cache, 0, 3)
    near_x = send(cache, 1, 0)
    back_y = send(cache, 0, 1)
    far_y = send(cache, 0, 2)
    near_xy = send(near_x, 0, 3)
    back_xy = send(back_y, 1, 0)
    far_xy = send(far_y, 1, 0)
    caches = [cache, near_y, far_y, back_y, near_x, near_xy, far_xy, back_xy]
    turned, last = pl.pallas_call(
        prep_kernel,
        out_shape=(
            jax.ShapeDtypeStruct((own, LANES), jnp.bfloat16),
            jax.ShapeDtypeStruct((RING // 2, 2 * HD, LANES), jnp.bfloat16),
        ),
        in_specs=[vmem()],
        out_specs=(vmem(), vmem()),
        cost_estimate=pl.CostEstimate(
            flops=1 << 20, bytes_accessed=1 << 22, transcendentals=0
        ),
        compiler_params=pltpu.CompilerParams(vmem_limit_bytes=VMEM_LIMIT),
        name="prep",
    )(mine)
    window = lax.ppermute(last, "seq", [(s, s + RING) for s in range(seq - RING)])
    buffers = [pltpu.VMEM((CH, QB), jnp.float32)] * 2 + [pltpu.VMEM((CH, QB), jnp.bfloat16)] * 2
    upper, stats, sums = pl.pallas_call(
        functools.partial(attend_kernel, rings=rings),
        out_shape=(
            jax.ShapeDtypeStruct((RING // 2, HD, BLK), jnp.bfloat16),
            jax.ShapeDtypeStruct((blocks // 2, 16, QB), jnp.float32),
            jax.ShapeDtypeStruct((blocks // 2, HD, QB), jnp.float32),
        ),
        in_specs=[smem()] + [vmem()] * (5 + rings),
        out_specs=(vmem(), vmem(), vmem()),
        scratch_shapes=[
            pltpu.VMEM((own + G * W, LANES), jnp.bfloat16),
            pltpu.VMEM(((own + G * W) // BLK, HD, BLK), jnp.bfloat16),
            *buffers,
        ],
        cost_estimate=pl.CostEstimate(
            flops=own * 2 * W * HD * 4, bytes_accessed=1 << 22, transcendentals=own * 2 * W
        ),
        compiler_params=pltpu.CompilerParams(vmem_limit_bytes=VMEM_LIMIT),
        name="attend",
    )(need, lows, sinks, mine_q, mine, turned, *caches)
    attn = pl.pallas_call(
        window_kernel,
        out_shape=jax.ShapeDtypeStruct((RING, HD, BLK), jnp.bfloat16),
        in_specs=[smem()] + [vmem()] * 6,
        out_specs=vmem(),
        scratch_shapes=[
            pltpu.VMEM((W, LANES), jnp.bfloat16),
            pltpu.VMEM((W // BLK, HD, BLK), jnp.bfloat16),
            *buffers,
        ],
        compiler_params=pltpu.CompilerParams(vmem_limit_bytes=VMEM_LIMIT),
        name="window",
    )(need, lows, mine_q, window, upper, stats, sums)
    attn_t = trade(attn, members).reshape(width, rows)
    give = project(1 - half, attn_t, w_out, jnp.bfloat16)
    got = lax.ppermute(give, "head", [(0, 1), (1, 0)])
    keep = project(half, attn_t, w_out, jnp.float32)
    return (keep + got.astype(jnp.float32)).astype(jnp.bfloat16)


def solution(mesh):
    placed = (
        P("seq", "head"),
        P("seq", "head"),
        P("seq", "head"),
        P("seq", "head"),
        P("seq", "head"),
        P(None, "head"),
        P(None, "head"),
        P(),
        P(),
        P("head", None),
    )
    return jax.shard_map(
        shards, mesh=mesh, in_specs=placed, out_specs=P("head", "seq"), check_vma=False
    )
```

```python
import functools
import math

import jax
import jax.numpy as jnp
from jax import lax
from jax.experimental import pallas as pl
from jax.experimental.pallas import tpu as pltpu
from jax.sharding import PartitionSpec as P

HD = 96
W = 1024
SINKS = 4
G = 2
RING = 16
BLK = 128
QB = 256
CH = 256
LANES = 128
FAR = 1 << 28
LOW = -1e30
VMEM_LIMIT = 24 << 20
PIECE = 256


def pack_kernel(k_ref, v_ref, ck_ref, cv_ref, out_ref):
    heads = k_ref.shape[1] // HD
    for which, ref in enumerate((k_ref, v_ref)):
        turned = ref[...].T
        for p in range(heads):
            out_ref[p, which * HD : (which + 1) * HD, :] = turned[p * HD : (p + 1) * HD, :]
    rows = ck_ref.shape[0]
    fill = jnp.zeros((rows, LANES - HD), ck_ref.dtype)
    for which, ref in enumerate((ck_ref, cv_ref)):
        for p in range(heads):
            piece = jnp.concatenate([ref[:, p * HD : (p + 1) * HD], fill], axis=1)
            base = 2 * HD + which * rows
            out_ref[p, base : base + rows, :] = piece


def gather_facts(place, lengths, groups, need, blocks):
    base = place[0] * RING * BLK
    own = RING * BLK
    for b in range((1 + G) * blocks):
        need[b] = FAR
    need[(1 + G) * blocks] = place[0]

    def one_request(r, carry):
        start, start_col, group_col = carry
        length = lengths[r]
        group = groups[r]
        first = jnp.where(start < base, 0, (start - base) // QB)
        last = jnp.minimum((start + length - 1 - base) // QB, blocks - 1)

        def mark(b, _):
            need[b] = jnp.minimum(need[b], start)
            offset = jnp.maximum(base + b * QB - start, 0)
            at = (1 + group) * blocks + b
            need[at] = jnp.minimum(need[at], offset)
            return 0

        @pl.when((start < base + own) & (start + length > base))
        def _():
            lax.fori_loop(first, last + 1, mark, 0)

        row = lax.broadcasted_iota(jnp.int32, start_col.shape, 0)
        start_col = jnp.where(row == r, start, start_col)
        group_col = jnp.where(row == r, group, group_col)
        return (start + length, start_col, group_col)

    reqs = lengths.shape[0]
    column = jnp.zeros((reqs, QB), jnp.int32)
    _, start_col, group_col = lax.fori_loop(0, reqs, one_request, (jnp.int32(0), column, column))
    return base, start_col, group_col


def query_facts(index, start_col, group_col):
    begun = start_col <= index
    start_q = jnp.max(jnp.where(begun, start_col, 0), axis=0, keepdims=True)
    here = begun & (start_col == start_q)
    group_q = jnp.max(jnp.where(here, group_col, 0), axis=0, keepdims=True)
    return jnp.maximum(start_q, index - (W - 1)), index - start_q, group_q


def turn(piece):
    pad = jnp.zeros((LANES - HD, BLK), jnp.bfloat16)
    return jnp.concatenate([piece, pad], axis=0).T


def query_block(query_ref, b):
    q_t = jnp.concatenate([query_ref[2 * b], query_ref[2 * b + 1]], axis=1)
    return jnp.concatenate([q_t, jnp.zeros((LANES - HD, QB), jnp.bfloat16)], axis=0)


def values(val_ref, at):
    slot = at // BLK
    return jnp.concatenate([val_ref[slot], val_ref[slot + 1]], axis=1)


def dot(a, b):
    return jnp.dot(a, b, preferred_element_type=jnp.float32)


FACTOR = (1.0 / math.sqrt(HD)) * math.log2(math.e)


def prep_kernel(own_ref, key_ref, last_ref):
    for j in range(RING // 2):
        last_ref[j] = own_ref[RING // 2 + j, 0 : 2 * HD, :]
    for j in range(RING):
        key_ref[j * BLK : (j + 1) * BLK, :] = turn(own_ref[j, 0:HD, :])


def pack_query_kernel(
    place, lengths, groups, q_ref, sk_ref, sv_ref, query_ref, sink_ref, low_ref, need
):
    turned = q_ref[...].T
    for p in range(q_ref.shape[1] // HD):
        query_ref[p] = turned[p * HD : (p + 1) * HD, :]
    width = sk_ref.shape[1]
    column = lax.broadcasted_iota(jnp.int32, (width, LANES), 0)
    lane = lax.broadcasted_iota(jnp.int32, (width, LANES), 1)
    pick = ((column == place[1] * HD + lane) & (lane < HD)).astype(jnp.float32).astype(jnp.bfloat16)
    for which, ref in enumerate((sk_ref, sv_ref)):
        piece = jnp.dot(ref[...], pick, preferred_element_type=jnp.float32)
        piece = jnp.concatenate([piece, jnp.zeros_like(piece)], axis=0)
        sink_ref[which * 16 : (which + 1) * 16, :] = piece.astype(jnp.bfloat16)
    own = RING * BLK
    blocks = own // QB
    cache_at = own
    base, start_col, group_col = gather_facts(place, lengths, groups, need, blocks)
    lane = lax.broadcasted_iota(jnp.int32, (1, QB), 1)
    for b in range(blocks):
        index = base + b * QB + lane
        low_q, offset, group_q = query_facts(index, start_col, group_col)
        low_ref[b, 0:1, :] = low_q - base
        for g in range(G):
            low_ref[b, 1 + g : 2 + g, :] = jnp.where(
                group_q == g, cache_at + g * W + offset + 1, FAR
            )
        low_ref[b, 1 + G : 2 + G, :] = jnp.full((1, QB), FAR, jnp.int32)
        low_ref[b, 2 + G : 3 + G, :] = group_q


def fold(rows, how):
    return how(rows.reshape(rows.shape[0] // 8, 8, QB), axis=0)


def visit(total, where_is, key_ref, val_ref, low_of, q_t, state, buffers):
    s_even, s_odd, p_even, p_odd = buffers
    row_iota = lax.broadcasted_iota(jnp.int32, (PIECE, QB), 0)
    pieces = [slice(n * PIECE, (n + 1) * PIECE) for n in range(CH // PIECE)]

    def scores(j, ref):
        at, kind = where_is(j)
        low = low_of(kind) - at
        peak = None
        for n, rows in enumerate(pieces):
            s = dot(key_ref[pl.ds(at + n * PIECE, PIECE), :], q_t)
            s = jnp.where(row_iota >= low - n * PIECE, s, LOW)
            ref[rows, :] = s
            high = fold(s, jnp.max)
            peak = high if peak is None else jnp.maximum(peak, high)
        return peak, at

    def weigh(s_ref, p_ref, peak, top, den):
        new = jnp.maximum(top, jnp.max(peak, axis=0, keepdims=True))
        fade = jnp.exp2((top - new) * FACTOR)
        den = den * fade
        for rows in pieces:
            p = jnp.exp2((s_ref[rows, :] - new) * FACTOR)
            den = den + fold(p, jnp.sum)
            p_ref[rows, :] = p.astype(jnp.bfloat16)
        return new, fade, den

    top, den, acc, before = state
    peak, at = scores(0, s_even)

    def step(j, state):
        top, den, acc, before, peak, at = state
        next_peak, next_at = scores(2 * j + 1, s_odd)
        acc = acc + dot(values(val_ref, before), p_odd[...])
        top, fade, den = weigh(s_even, p_even, peak, top, den)
        acc = acc * fade + dot(values(val_ref, at), p_even[...])
        peak, last_at = scores(2 * j + 2, s_even)
        top, fade, den = weigh(s_odd, p_odd, next_peak, top, den)
        acc = acc * fade
        return (top, den, acc, next_at, peak, last_at)

    top, den, acc, before, _, _ = lax.fori_loop(
        0, (total + 1) // 2, step, (top, den, acc, before, peak, at)
    )
    return top, den, acc + dot(values(val_ref, before), p_odd[...])


def visit_plain(total, where_is, key_ref, val_ref, low_of, q_t, state):
    row_iota = lax.broadcasted_iota(jnp.int32, (CH, QB), 0)

    def step(j, state):
        top, den, acc = state
        scores, ats = [], []
        for u in range(2):
            at, kind = where_is(2 * j + u)
            s = dot(key_ref[pl.ds(at, CH), :], q_t)
            scores.append(jnp.where(row_iota >= low_of(kind) - at, s, LOW))
            ats.append(at)
        peak = jnp.maximum(fold(scores[0], jnp.max), fold(scores[1], jnp.max))
        new = jnp.maximum(top, jnp.max(peak, axis=0, keepdims=True))
        fade = jnp.exp2((top - new) * FACTOR)
        den = den * fade
        ps = []
        for u in range(2):
            p = jnp.exp2((scores[u] - new) * FACTOR)
            den = den + fold(p, jnp.sum)
            ps.append(p.astype(jnp.bfloat16))
        vals = jnp.concatenate([values(val_ref, at) for at in ats], axis=1)
        acc = acc * fade + dot(vals, jnp.concatenate(ps, axis=0))
        return (new, den, acc)

    return lax.fori_loop(0, (total + 1) // 2, step, state)


def attend_kernel(
    need, low_ref, sink_ref, query_ref, own_ref, turned_ref, *rest, rings
):
    caches = rest[:rings]
    upper_ref, stat_ref, acc_ref, key_ref, val_ref = rest[rings : rings + 5]
    buffers = rest[rings + 5 :]
    own = RING * BLK
    blocks = own // QB
    ring = need[(1 + G) * blocks]
    base = ring * own
    key_ref[0:own, :] = turned_ref[...]
    for j in range(RING):
        val_ref[j] = own_ref[j, HD : 2 * HD, :]
    rows = RING * 16
    for k in range(rings):
        source = lax.rem(lax.rem(ring, 4) + k % 4, 4) + 4 * lax.rem(ring // 4 + k // 4, 2)
        piece = caches[k][...]
        at = pl.multiple_of(own + source * rows, rows)
        key_ref[pl.ds(at, rows), :] = piece[:, 0:16, :].reshape(rows, LANES)
        turned = piece[:, 16:32, :].reshape(rows, LANES).T
        for half in range(rows // BLK):
            val_ref[at // BLK + half] = turned[0:HD, half * BLK : (half + 1) * BLK]
    lane = lax.broadcasted_iota(jnp.int32, (1, QB), 1)
    row_iota = lax.broadcasted_iota(jnp.int32, (CH, QB), 0)
    sink_row = lax.broadcasted_iota(jnp.int32, (16, QB), 0)
    sink_v = sink_ref[16:32, :].T[0:HD, :]

    def one_block(b, _):
        low_suffix = low_ref[b, 0:1, :]
        group_q = low_ref[b, 2 + G : 3 + G, :]
        q_t = query_block(query_ref, b)
        at0 = pl.multiple_of(b * QB, CH)
        s_d = dot(key_ref[pl.ds(at0, CH), :], q_t)
        s_d = jnp.where((row_iota >= low_suffix - at0) & (row_iota <= lane), s_d, LOW)
        s_s = dot(sink_ref[0:16, :], q_t)
        s_s = jnp.where((sink_row // SINKS == group_q) & (sink_row < G * SINKS), s_s, LOW)
        top = jnp.maximum(jnp.max(s_d, axis=0, keepdims=True), jnp.max(s_s, axis=0, keepdims=True))
        p_d = jnp.exp2((s_d - top) * FACTOR)
        p_s = jnp.exp2((s_s - top) * FACTOR)
        den = fold(p_d, jnp.sum) + fold(p_s, jnp.sum)
        buffers[3][...] = p_d.astype(jnp.bfloat16)
        acc = dot(sink_v, p_s.astype(jnp.bfloat16))

        first = jnp.maximum(jnp.maximum(need[b] - base, b * QB - (W - 1)), 0) // CH
        n_suffix = b - first
        c0 = [jnp.minimum((need[(1 + g) * blocks + b] + 1) // CH, W // CH) for g in range(G)]
        n0, n1 = [W // CH - c for c in c0]
        total = n_suffix + n0 + n1

        def where_is(j):
            in0 = j - n_suffix
            in1 = in0 - n0
            at = jnp.where(
                in0 < 0,
                (first + j) * CH,
                jnp.where(
                    in1 < 0,
                    own + (c0[0] + in0) * CH,
                    jnp.where(j < total, own + W + (c0[1] + in1) * CH, 0),
                ),
            )
            kind = jnp.where(in0 < 0, 0, jnp.where(in1 < 0, 1, jnp.where(j < total, 2, 3)))
            return pl.multiple_of(at, CH), kind

        def low_of(kind):
            return low_ref[b, pl.ds(kind, 1), :]

        state = (top, den, acc, at0)
        top, den, acc = visit(total, where_is, key_ref, val_ref, low_of, q_t, state, buffers)

        @pl.when(b < blocks // 2)
        def _():
            stat_ref[b, 0:8, :] = jnp.broadcast_to(top, (8, QB))
            stat_ref[b, 8:16, :] = den
            acc_ref[b] = acc

        @pl.when(b >= blocks // 2)
        def _():
            done = (acc / jnp.sum(den, axis=0, keepdims=True)).astype(jnp.bfloat16)
            upper_ref[2 * b - RING // 2] = done[:, 0:BLK]
            upper_ref[2 * b + 1 - RING // 2] = done[:, BLK:QB]

        return 0

    lax.fori_loop(0, blocks, one_block, 0)


def window_kernel(
    need, low_ref, query_ref, win_ref, upper_ref, stat_ref, acc_ref, out_ref,
    key_ref, val_ref,
):
    blocks = RING * BLK // QB
    base = need[(1 + G) * blocks] * RING * BLK
    for j in range(RING // 2):
        key_ref[j * BLK : (j + 1) * BLK, :] = turn(win_ref[j, 0:HD, :])
        val_ref[j] = win_ref[j, HD : 2 * HD, :]
        out_ref[RING // 2 + j] = upper_ref[j]

    def one_block(b, _):
        q_t = query_block(query_ref, b)
        first = jnp.maximum(need[b] - base, b * QB - (W - 1)) + W
        first = jnp.minimum(first // CH, W // CH)
        total = W // CH - first

        def where_is(j):
            at = jnp.where(j < total, (first + j) * CH, 0)
            return pl.multiple_of(at, CH), jnp.where(j < total, 0, 1 + G)

        def low_of(kind):
            return low_ref[b, pl.ds(kind, 1), :] + jnp.where(kind == 0, W, 0)

        state = (stat_ref[b, 0:1, :], stat_ref[b, 8:16, :], acc_ref[b])
        _, den, acc = visit_plain(total, where_is, key_ref, val_ref, low_of, q_t, state)
        done = (acc / jnp.sum(den, axis=0, keepdims=True)).astype(jnp.bfloat16)
        out_ref[2 * b] = done[:, 0:BLK]
        out_ref[2 * b + 1] = done[:, BLK:QB]
        return 0

    lax.fori_loop(0, blocks // 2, one_block, 0)


def project_kernel(side, attn_ref, w_ref, out_ref, half_ref, sum_ref, arrived):
    features = half_ref.shape[1]
    columns = pl.ds(pl.multiple_of(side[0] * features, features), features)
    parts = arrived.shape[0]
    tall = half_ref.shape[0] // parts
    loads = []
    for n in range(parts):
        rows = pl.ds(n * tall, tall)
        loads.append(
            pltpu.make_async_copy(w_ref.at[rows, columns], half_ref.at[rows, :], arrived.at[n])
        )
    for load in loads:
        load.start()
    turned = attn_ref[...].T
    for n in range(parts):
        loads[n].wait()
        at = slice(n * tall, (n + 1) * tall)
        part = dot(turned[:, at], half_ref[at, :])
        if n == 0:
            sum_ref[...] = part
        elif n < parts - 1:
            sum_ref[...] += part
        else:
            out_ref[...] = (sum_ref[...] + part).T.astype(out_ref.dtype)


def project(side, attn_t, w_out, dtype):
    width, rows = attn_t.shape
    features = w_out.shape[1] // 2
    return pl.pallas_call(
        project_kernel,
        out_shape=jax.ShapeDtypeStruct((features, rows), dtype),
        in_specs=[smem(), vmem(), pl.BlockSpec(memory_space=pltpu.HBM)],
        out_specs=vmem(),
        scratch_shapes=[
            pltpu.VMEM((width, features), jnp.bfloat16),
            pltpu.VMEM((rows, features), jnp.float32),
            pltpu.SemaphoreType.DMA((6,)),
        ],
        cost_estimate=pl.CostEstimate(
            flops=2 * width * features * rows,
            bytes_accessed=2 * width * features,
            transcendentals=0,
        ),
        compiler_params=pltpu.CompilerParams(vmem_limit_bytes=50 << 20),
        name="project",
    )(side.reshape(1), attn_t, w_out)


def vmem():
    return pl.BlockSpec(memory_space=pltpu.VMEM)


def smem():
    return pl.BlockSpec(memory_space=pltpu.SMEM)


def shards(
    queries, keys, values, cache_k, cache_v, sink_k, sink_v, suffix_lengths, request_group, w_out
):
    rows, width = queries.shape
    heads = width // HD
    seq = lax.axis_size("seq")
    rings = seq // RING
    device = lax.axis_index("seq")
    half = lax.axis_index("head")
    packed = pl.pallas_call(
        pack_kernel,
        out_shape=jax.ShapeDtypeStruct((heads, 2 * HD + 32, LANES), jnp.bfloat16),
        in_specs=[vmem()] * 4,
        out_specs=vmem(),
        name="pack",
    )(keys, values, cache_k, cache_v)
    own = RING * BLK
    blocks = own // QB
    place = jnp.stack([device // RING, device % RING]).astype(jnp.int32)
    packed_q, sinks, lows, need = pl.pallas_call(
        pack_query_kernel,
        out_shape=(
            jax.ShapeDtypeStruct((heads, HD, LANES), jnp.bfloat16),
            jax.ShapeDtypeStruct((32, LANES), jnp.bfloat16),
            jax.ShapeDtypeStruct((blocks, 8, QB), jnp.int32),
            jax.ShapeDtypeStruct(((1 + G) * blocks + 1,), jnp.int32),
        ),
        in_specs=[smem()] * 3 + [vmem()] * 3,
        out_specs=(vmem(), vmem(), vmem(), smem()),
        cost_estimate=pl.CostEstimate(flops=1 << 20, bytes_accessed=1 << 21, transcendentals=0),
        compiler_params=pltpu.CompilerParams(vmem_limit_bytes=VMEM_LIMIT),
        name="pack_query",
    )(place, suffix_lengths, request_group, queries, sink_k, sink_v)
    members = [[r * RING + i for i in range(RING)] for r in range(rings)]

    def trade(array, groups):
        return lax.all_to_all(array, "seq", 0, 0, axis_index_groups=groups, tiled=True)

    mine = trade(packed, members)
    mine_q = trade(packed_q, members)
    cache = mine[:, 2 * HD :, :]

    def send(array, dx, dy):
        pairs = []
        for r in range(rings):
            to = (r % 4 + dy) % 4 + 4 * ((r // 4 + dx) % 2)
            pairs += [(r * RING + i, to * RING + i) for i in range(RING)]
        return lax.ppermute(array, "seq", pairs)

    near_y = send(cache, 0, 3)
    near_x = send(cache, 1, 0)
    back_y = send(cache, 0, 1)
    far_y = send(cache, 0, 2)
    near_xy = send(near_x, 0, 3)
    back_xy = send(back_y, 1, 0)
    far_xy = send(far_y, 1, 0)
    caches = [cache, near_y, far_y, back_y, near_x, near_xy, far_xy, back_xy]
    turned, last = pl.pallas_call(
        prep_kernel,
        out_shape=(
            jax.ShapeDtypeStruct((own, LANES), jnp.bfloat16),
            jax.ShapeDtypeStruct((RING // 2, 2 * HD, LANES), jnp.bfloat16),
        ),
        in_specs=[vmem()],
        out_specs=(vmem(), vmem()),
        cost_estimate=pl.CostEstimate(
            flops=1 << 20, bytes_accessed=1 << 22, transcendentals=0
        ),
        compiler_params=pltpu.CompilerParams(vmem_limit_bytes=VMEM_LIMIT),
        name="prep",
    )(mine)
    window = lax.ppermute(last, "seq", [(s, s + RING) for s in range(seq - RING)])
    buffers = [pltpu.VMEM((CH, QB), jnp.float32)] * 2 + [pltpu.VMEM((CH, QB), jnp.bfloat16)] * 2
    upper, stats, sums = pl.pallas_call(
        functools.partial(attend_kernel, rings=rings),
        out_shape=(
            jax.ShapeDtypeStruct((RING // 2, HD, BLK), jnp.bfloat16),
            jax.ShapeDtypeStruct((blocks // 2, 16, QB), jnp.float32),
            jax.ShapeDtypeStruct((blocks // 2, HD, QB), jnp.float32),
        ),
        in_specs=[smem()] + [vmem()] * (5 + rings),
        out_specs=(vmem(), vmem(), vmem()),
        scratch_shapes=[
            pltpu.VMEM((own + G * W, LANES), jnp.bfloat16),
            pltpu.VMEM(((own + G * W) // BLK, HD, BLK), jnp.bfloat16),
            *buffers,
        ],
        cost_estimate=pl.CostEstimate(
            flops=own * 2 * W * HD * 4, bytes_accessed=1 << 22, transcendentals=own * 2 * W
        ),
        compiler_params=pltpu.CompilerParams(vmem_limit_bytes=VMEM_LIMIT),
        name="attend",
    )(need, lows, sinks, mine_q, mine, turned, *caches)
    attn = pl.pallas_call(
        window_kernel,
        out_shape=jax.ShapeDtypeStruct((RING, HD, BLK), jnp.bfloat16),
        in_specs=[smem()] + [vmem()] * 6,
        out_specs=vmem(),
        scratch_shapes=[
            pltpu.VMEM((W, LANES), jnp.bfloat16),
            pltpu.VMEM((W // BLK, HD, BLK), jnp.bfloat16),
        ],
        compiler_params=pltpu.CompilerParams(vmem_limit_bytes=VMEM_LIMIT),
        name="window",
    )(need, lows, mine_q, window, upper, stats, sums)
    attn_t = trade(attn, members).reshape(width, rows)
    give = project(1 - half, attn_t, w_out, jnp.bfloat16)
    got = lax.ppermute(give, "head", [(0, 1), (1, 0)])
    keep = project(half, attn_t, w_out, jnp.float32)
    return (keep + got.astype(jnp.float32)).astype(jnp.bfloat16)


def solution(mesh):
    placed = (
        P("seq", "head"),
        P("seq", "head"),
        P("seq", "head"),
        P("seq", "head"),
        P("seq", "head"),
        P(None, "head"),
        P(None, "head"),
        P(),
        P(),
        P("head", None),
    )
    return jax.shard_map(
        shards, mesh=mesh, in_specs=placed, out_specs=P("head", "seq"), check_vma=False
    )
```

```python
import functools
import math

import jax
import jax.numpy as jnp
from jax import lax
from jax.experimental import pallas as pl
from jax.experimental.pallas import tpu as pltpu
from jax.sharding import PartitionSpec as P

HD = 96
W = 1024
SINKS = 4
G = 2
RING = 16
BLK = 128
QB = 256
CH = 256
LANES = 128
FAR = 1 << 28
LOW = -1e30
VMEM_LIMIT = 24 << 20
PIECE = 256


def pack_kernel(k_ref, v_ref, ck_ref, cv_ref, out_ref):
    heads = k_ref.shape[1] // HD
    for which, ref in enumerate((k_ref, v_ref)):
        turned = ref[...].T
        for p in range(heads):
            out_ref[p, which * HD : (which + 1) * HD, :] = turned[p * HD : (p + 1) * HD, :]
    rows = ck_ref.shape[0]
    fill = jnp.zeros((rows, LANES - HD), ck_ref.dtype)
    for which, ref in enumerate((ck_ref, cv_ref)):
        for p in range(heads):
            piece = jnp.concatenate([ref[:, p * HD : (p + 1) * HD], fill], axis=1)
            base = 2 * HD + which * rows
            out_ref[p, base : base + rows, :] = piece


def gather_facts(place, lengths, groups, need, blocks):
    base = place[0] * RING * BLK
    own = RING * BLK
    for b in range((1 + G) * blocks):
        need[b] = FAR
    need[(1 + G) * blocks] = place[0]

    def one_request(r, carry):
        start, start_col, group_col = carry
        length = lengths[r]
        group = groups[r]
        first = jnp.where(start < base, 0, (start - base) // QB)
        last = jnp.minimum((start + length - 1 - base) // QB, blocks - 1)

        def mark(b, _):
            need[b] = jnp.minimum(need[b], start)
            offset = jnp.maximum(base + b * QB - start, 0)
            at = (1 + group) * blocks + b
            need[at] = jnp.minimum(need[at], offset)
            return 0

        @pl.when((start < base + own) & (start + length > base))
        def _():
            lax.fori_loop(first, last + 1, mark, 0)

        row = lax.broadcasted_iota(jnp.int32, start_col.shape, 0)
        start_col = jnp.where(row == r, start, start_col)
        group_col = jnp.where(row == r, group, group_col)
        return (start + length, start_col, group_col)

    reqs = lengths.shape[0]
    column = jnp.zeros((reqs, QB), jnp.int32)
    _, start_col, group_col = lax.fori_loop(0, reqs, one_request, (jnp.int32(0), column, column))
    return base, start_col, group_col


def query_facts(index, start_col, group_col):
    begun = start_col <= index
    start_q = jnp.max(jnp.where(begun, start_col, 0), axis=0, keepdims=True)
    here = begun & (start_col == start_q)
    group_q = jnp.max(jnp.where(here, group_col, 0), axis=0, keepdims=True)
    return jnp.maximum(start_q, index - (W - 1)), index - start_q, group_q


def turn(piece):
    pad = jnp.zeros((LANES - HD, BLK), jnp.bfloat16)
    return jnp.concatenate([piece, pad], axis=0).T


def query_block(query_ref, b):
    q_t = jnp.concatenate([query_ref[2 * b], query_ref[2 * b + 1]], axis=1)
    return jnp.concatenate([q_t, jnp.zeros((LANES - HD, QB), jnp.bfloat16)], axis=0)


def values(val_ref, at):
    slot = at // BLK
    return jnp.concatenate([val_ref[slot], val_ref[slot + 1]], axis=1)


def dot(a, b):
    return jnp.dot(a, b, preferred_element_type=jnp.float32)


FACTOR = (1.0 / math.sqrt(HD)) * math.log2(math.e)


def prep_kernel(own_ref, key_ref, last_ref):
    for j in range(RING // 2):
        last_ref[j] = own_ref[RING // 2 + j, 0 : 2 * HD, :]
    for j in range(RING):
        key_ref[j * BLK : (j + 1) * BLK, :] = turn(own_ref[j, 0:HD, :])


def pack_query_kernel(
    place, lengths, groups, q_ref, sk_ref, sv_ref, query_ref, sink_ref, low_ref, need
):
    turned = q_ref[...].T
    for p in range(q_ref.shape[1] // HD):
        query_ref[p] = turned[p * HD : (p + 1) * HD, :]
    width = sk_ref.shape[1]
    column = lax.broadcasted_iota(jnp.int32, (width, LANES), 0)
    lane = lax.broadcasted_iota(jnp.int32, (width, LANES), 1)
    pick = ((column == place[1] * HD + lane) & (lane < HD)).astype(jnp.float32).astype(jnp.bfloat16)
    for which, ref in enumerate((sk_ref, sv_ref)):
        piece = jnp.dot(ref[...], pick, preferred_element_type=jnp.float32)
        piece = jnp.concatenate([piece, jnp.zeros_like(piece)], axis=0)
        sink_ref[which * 16 : (which + 1) * 16, :] = piece.astype(jnp.bfloat16)
    own = RING * BLK
    blocks = own // QB
    cache_at = own
    base, start_col, group_col = gather_facts(place, lengths, groups, need, blocks)
    lane = lax.broadcasted_iota(jnp.int32, (1, QB), 1)
    for b in range(blocks):
        index = base + b * QB + lane
        low_q, offset, group_q = query_facts(index, start_col, group_col)
        low_ref[b, 0:1, :] = low_q - base
        for g in range(G):
            low_ref[b, 1 + g : 2 + g, :] = jnp.where(
                group_q == g, cache_at + g * W + offset + 1, FAR
            )
        low_ref[b, 1 + G : 2 + G, :] = jnp.full((1, QB), FAR, jnp.int32)
        low_ref[b, 2 + G : 3 + G, :] = group_q


def fold(rows, how):
    return how(rows.reshape(rows.shape[0] // 8, 8, QB), axis=0)


def visit(total, where_is, key_ref, val_ref, low_of, q_t, state, buffers):
    s_even, s_odd, p_even, p_odd = buffers
    row_iota = lax.broadcasted_iota(jnp.int32, (PIECE, QB), 0)
    pieces = [slice(n * PIECE, (n + 1) * PIECE) for n in range(CH // PIECE)]

    def scores(j, ref):
        at, kind = where_is(j)
        low = low_of(kind) - at
        peak = None
        for n, rows in enumerate(pieces):
            s = dot(key_ref[pl.ds(at + n * PIECE, PIECE), :], q_t)
            s = jnp.where(row_iota >= low - n * PIECE, s, LOW)
            ref[rows, :] = s
            high = fold(s, jnp.max)
            peak = high if peak is None else jnp.maximum(peak, high)
        return peak, at

    def weigh(s_ref, p_ref, peak, top, den):
        new = jnp.maximum(top, jnp.max(peak, axis=0, keepdims=True))
        fade = jnp.exp2((top - new) * FACTOR)
        den = den * fade
        for rows in pieces:
            p = jnp.exp2((s_ref[rows, :] - new) * FACTOR)
            den = den + fold(p, jnp.sum)
            p_ref[rows, :] = p.astype(jnp.bfloat16)
        return new, fade, den

    top, den, acc, before = state
    peak, at = scores(0, s_even)

    def step(j, state):
        top, den, acc, before, peak, at = state
        next_peak, next_at = scores(2 * j + 1, s_odd)
        acc = acc + dot(values(val_ref, before), p_odd[...])
        top, fade, den = weigh(s_even, p_even, peak, top, den)
        acc = acc * fade + dot(values(val_ref, at), p_even[...])
        peak, last_at = scores(2 * j + 2, s_even)
        top, fade, den = weigh(s_odd, p_odd, next_peak, top, den)
        acc = acc * fade
        return (top, den, acc, next_at, peak, last_at)

    top, den, acc, before, _, _ = lax.fori_loop(
        0, (total + 1) // 2, step, (top, den, acc, before, peak, at)
    )
    return top, den, acc + dot(values(val_ref, before), p_odd[...])


def visit_plain(total, where_is, key_ref, val_ref, low_of, q_t, state):
    row_iota = lax.broadcasted_iota(jnp.int32, (CH, QB), 0)

    def step(j, state):
        top, den, acc = state
        scores, ats = [], []
        for u in range(2):
            at, kind = where_is(2 * j + u)
            s = dot(key_ref[pl.ds(at, CH), :], q_t)
            scores.append(jnp.where(row_iota >= low_of(kind) - at, s, LOW))
            ats.append(at)
        peak = jnp.maximum(fold(scores[0], jnp.max), fold(scores[1], jnp.max))
        new = jnp.maximum(top, jnp.max(peak, axis=0, keepdims=True))
        fade = jnp.exp2((top - new) * FACTOR)
        den = den * fade
        ps = []
        for u in range(2):
            p = jnp.exp2((scores[u] - new) * FACTOR)
            den = den + fold(p, jnp.sum)
            ps.append(p.astype(jnp.bfloat16))
        vals = jnp.concatenate([values(val_ref, at) for at in ats], axis=1)
        acc = acc * fade + dot(vals, jnp.concatenate(ps, axis=0))
        return (new, den, acc)

    return lax.fori_loop(0, (total + 1) // 2, step, state)


def attend_kernel(
    need, low_ref, sink_ref, query_ref, own_ref, turned_ref, *rest, rings
):
    caches = rest[:rings]
    upper_ref, stat_ref, acc_ref, key_ref, val_ref = rest[rings : rings + 5]
    buffers = rest[rings + 5 :]
    own = RING * BLK
    blocks = own // QB
    ring = need[(1 + G) * blocks]
    base = ring * own
    key_ref[0:own, :] = turned_ref[...]
    for j in range(RING):
        val_ref[j] = own_ref[j, HD : 2 * HD, :]
    rows = RING * 16
    for k in range(rings):
        source = lax.rem(lax.rem(ring, 4) + k % 4, 4) + 4 * lax.rem(ring // 4 + k // 4, 2)
        piece = caches[k][...]
        at = pl.multiple_of(own + source * rows, rows)
        key_ref[pl.ds(at, rows), :] = piece[:, 0:16, :].reshape(rows, LANES)
        turned = piece[:, 16:32, :].reshape(rows, LANES).T
        for half in range(rows // BLK):
            val_ref[at // BLK + half] = turned[0:HD, half * BLK : (half + 1) * BLK]
    lane = lax.broadcasted_iota(jnp.int32, (1, QB), 1)
    row_iota = lax.broadcasted_iota(jnp.int32, (CH, QB), 0)
    sink_row = lax.broadcasted_iota(jnp.int32, (16, QB), 0)
    sink_v = sink_ref[16:32, :].T[0:HD, :]

    def one_block(b):
        low_suffix = low_ref[b, 0:1, :]
        group_q = low_ref[b, 2 + G : 3 + G, :]
        q_t = query_block(query_ref, b)
        at0 = pl.multiple_of(b * QB, CH)
        s_d = dot(key_ref[pl.ds(at0, CH), :], q_t)
        s_d = jnp.where((row_iota >= low_suffix - at0) & (row_iota <= lane), s_d, LOW)
        s_s = dot(sink_ref[0:16, :], q_t)
        s_s = jnp.where((sink_row // SINKS == group_q) & (sink_row < G * SINKS), s_s, LOW)
        top = jnp.maximum(jnp.max(s_d, axis=0, keepdims=True), jnp.max(s_s, axis=0, keepdims=True))
        p_d = jnp.exp2((s_d - top) * FACTOR)
        p_s = jnp.exp2((s_s - top) * FACTOR)
        den = fold(p_d, jnp.sum) + fold(p_s, jnp.sum)
        buffers[3][...] = p_d.astype(jnp.bfloat16)
        acc = dot(sink_v, p_s.astype(jnp.bfloat16))

        first = jnp.maximum(jnp.maximum(need[b] - base, b * QB - (W - 1)), 0) // CH
        n_suffix = b - first
        c0 = [jnp.minimum((need[(1 + g) * blocks + b] + 1) // CH, W // CH) for g in range(G)]
        n0, n1 = [W // CH - c for c in c0]
        total = n_suffix + n0 + n1

        def where_is(j):
            in0 = j - n_suffix
            in1 = in0 - n0
            at = jnp.where(
                in0 < 0,
                (first + j) * CH,
                jnp.where(
                    in1 < 0,
                    own + (c0[0] + in0) * CH,
                    jnp.where(j < total, own + W + (c0[1] + in1) * CH, 0),
                ),
            )
            kind = jnp.where(in0 < 0, 0, jnp.where(in1 < 0, 1, jnp.where(j < total, 2, 3)))
            return pl.multiple_of(at, CH), kind

        def low_of(kind):
            return low_ref[b, pl.ds(kind, 1), :]

        state = (top, den, acc, at0)
        top, den, acc = visit(total, where_is, key_ref, val_ref, low_of, q_t, state, buffers)

        @pl.when(b < blocks // 2)
        def _():
            stat_ref[b, 0:8, :] = jnp.broadcast_to(top, (8, QB))
            stat_ref[b, 8:16, :] = den
            acc_ref[b] = acc

        @pl.when(b >= blocks // 2)
        def _():
            done = (acc / jnp.sum(den, axis=0, keepdims=True)).astype(jnp.bfloat16)
            upper_ref[2 * b - RING // 2] = done[:, 0:BLK]
            upper_ref[2 * b + 1 - RING // 2] = done[:, BLK:QB]

        return 0

    for b in range(blocks):
        one_block(b)


def window_kernel(
    need, low_ref, query_ref, win_ref, upper_ref, stat_ref, acc_ref, out_ref,
    key_ref, val_ref,
):
    blocks = RING * BLK // QB
    base = need[(1 + G) * blocks] * RING * BLK
    for j in range(RING // 2):
        key_ref[j * BLK : (j + 1) * BLK, :] = turn(win_ref[j, 0:HD, :])
        val_ref[j] = win_ref[j, HD : 2 * HD, :]
        out_ref[RING // 2 + j] = upper_ref[j]

    def one_block(b):
        q_t = query_block(query_ref, b)
        first = jnp.maximum(need[b] - base, b * QB - (W - 1)) + W
        first = jnp.minimum(first // CH, W // CH)
        total = W // CH - first

        def where_is(j):
            at = jnp.where(j < total, (first + j) * CH, 0)
            return pl.multiple_of(at, CH), jnp.where(j < total, 0, 1 + G)

        def low_of(kind):
            return low_ref[b, pl.ds(kind, 1), :] + jnp.where(kind == 0, W, 0)

        state = (stat_ref[b, 0:1, :], stat_ref[b, 8:16, :], acc_ref[b])
        _, den, acc = visit_plain(total, where_is, key_ref, val_ref, low_of, q_t, state)
        done = (acc / jnp.sum(den, axis=0, keepdims=True)).astype(jnp.bfloat16)
        out_ref[2 * b] = done[:, 0:BLK]
        out_ref[2 * b + 1] = done[:, BLK:QB]
        return 0

    for b in range(blocks // 2):
        one_block(b)


def project_kernel(side, attn_ref, w_ref, out_ref, half_ref, sum_ref, arrived):
    features = half_ref.shape[1]
    columns = pl.ds(pl.multiple_of(side[0] * features, features), features)
    parts = arrived.shape[0]
    tall = half_ref.shape[0] // parts
    loads = []
    for n in range(parts):
        rows = pl.ds(n * tall, tall)
        loads.append(
            pltpu.make_async_copy(w_ref.at[rows, columns], half_ref.at[rows, :], arrived.at[n])
        )
    for load in loads:
        load.start()
    turned = attn_ref[...].T
    for n in range(parts):
        loads[n].wait()
        at = slice(n * tall, (n + 1) * tall)
        part = dot(turned[:, at], half_ref[at, :])
        if n == 0:
            sum_ref[...] = part
        elif n < parts - 1:
            sum_ref[...] += part
        else:
            out_ref[...] = (sum_ref[...] + part).T.astype(out_ref.dtype)


def project(side, attn_t, w_out, dtype):
    width, rows = attn_t.shape
    features = w_out.shape[1] // 2
    return pl.pallas_call(
        project_kernel,
        out_shape=jax.ShapeDtypeStruct((features, rows), dtype),
        in_specs=[smem(), vmem(), pl.BlockSpec(memory_space=pltpu.HBM)],
        out_specs=vmem(),
        scratch_shapes=[
            pltpu.VMEM((width, features), jnp.bfloat16),
            pltpu.VMEM((rows, features), jnp.float32),
            pltpu.SemaphoreType.DMA((6,)),
        ],
        cost_estimate=pl.CostEstimate(
            flops=2 * width * features * rows,
            bytes_accessed=2 * width * features,
            transcendentals=0,
        ),
        compiler_params=pltpu.CompilerParams(vmem_limit_bytes=50 << 20),
        name="project",
    )(side.reshape(1), attn_t, w_out)


def vmem():
    return pl.BlockSpec(memory_space=pltpu.VMEM)


def smem():
    return pl.BlockSpec(memory_space=pltpu.SMEM)


def shards(
    queries, keys, values, cache_k, cache_v, sink_k, sink_v, suffix_lengths, request_group, w_out
):
    rows, width = queries.shape
    heads = width // HD
    seq = lax.axis_size("seq")
    rings = seq // RING
    device = lax.axis_index("seq")
    half = lax.axis_index("head")
    packed = pl.pallas_call(
        pack_kernel,
        out_shape=jax.ShapeDtypeStruct((heads, 2 * HD + 32, LANES), jnp.bfloat16),
        in_specs=[vmem()] * 4,
        out_specs=vmem(),
        name="pack",
    )(keys, values, cache_k, cache_v)
    own = RING * BLK
    blocks = own // QB
    place = jnp.stack([device // RING, device % RING]).astype(jnp.int32)
    packed_q, sinks, lows, need = pl.pallas_call(
        pack_query_kernel,
        out_shape=(
            jax.ShapeDtypeStruct((heads, HD, LANES), jnp.bfloat16),
            jax.ShapeDtypeStruct((32, LANES), jnp.bfloat16),
            jax.ShapeDtypeStruct((blocks, 8, QB), jnp.int32),
            jax.ShapeDtypeStruct(((1 + G) * blocks + 1,), jnp.int32),
        ),
        in_specs=[smem()] * 3 + [vmem()] * 3,
        out_specs=(vmem(), vmem(), vmem(), smem()),
        cost_estimate=pl.CostEstimate(flops=1 << 20, bytes_accessed=1 << 21, transcendentals=0),
        compiler_params=pltpu.CompilerParams(vmem_limit_bytes=VMEM_LIMIT),
        name="pack_query",
    )(place, suffix_lengths, request_group, queries, sink_k, sink_v)
    members = [[r * RING + i for i in range(RING)] for r in range(rings)]

    def trade(array, groups):
        return lax.all_to_all(array, "seq", 0, 0, axis_index_groups=groups, tiled=True)

    mine = trade(packed, members)
    mine_q = trade(packed_q, members)
    cache = mine[:, 2 * HD :, :]

    def send(array, dx, dy):
        pairs = []
        for r in range(rings):
            to = (r % 4 + dy) % 4 + 4 * ((r // 4 + dx) % 2)
            pairs += [(r * RING + i, to * RING + i) for i in range(RING)]
        return lax.ppermute(array, "seq", pairs)

    near_y = send(cache, 0, 3)
    near_x = send(cache, 1, 0)
    back_y = send(cache, 0, 1)
    far_y = send(cache, 0, 2)
    near_xy = send(near_x, 0, 3)
    back_xy = send(back_y, 1, 0)
    far_xy = send(far_y, 1, 0)
    caches = [cache, near_y, far_y, back_y, near_x, near_xy, far_xy, back_xy]
    turned, last = pl.pallas_call(
        prep_kernel,
        out_shape=(
            jax.ShapeDtypeStruct((own, LANES), jnp.bfloat16),
            jax.ShapeDtypeStruct((RING // 2, 2 * HD, LANES), jnp.bfloat16),
        ),
        in_specs=[vmem()],
        out_specs=(vmem(), vmem()),
        cost_estimate=pl.CostEstimate(
            flops=1 << 20, bytes_accessed=1 << 22, transcendentals=0
        ),
        compiler_params=pltpu.CompilerParams(vmem_limit_bytes=VMEM_LIMIT),
        name="prep",
    )(mine)
    window = lax.ppermute(last, "seq", [(s, s + RING) for s in range(seq - RING)])
    buffers = [pltpu.VMEM((CH, QB), jnp.float32)] * 2 + [pltpu.VMEM((CH, QB), jnp.bfloat16)] * 2
    upper, stats, sums = pl.pallas_call(
        functools.partial(attend_kernel, rings=rings),
        out_shape=(
            jax.ShapeDtypeStruct((RING // 2, HD, BLK), jnp.bfloat16),
            jax.ShapeDtypeStruct((blocks // 2, 16, QB), jnp.float32),
            jax.ShapeDtypeStruct((blocks // 2, HD, QB), jnp.float32),
        ),
        in_specs=[smem()] + [vmem()] * (5 + rings),
        out_specs=(vmem(), vmem(), vmem()),
        scratch_shapes=[
            pltpu.VMEM((own + G * W, LANES), jnp.bfloat16),
            pltpu.VMEM(((own + G * W) // BLK, HD, BLK), jnp.bfloat16),
            *buffers,
        ],
        cost_estimate=pl.CostEstimate(
            flops=own * 2 * W * HD * 4, bytes_accessed=1 << 22, transcendentals=own * 2 * W
        ),
        compiler_params=pltpu.CompilerParams(vmem_limit_bytes=VMEM_LIMIT),
        name="attend",
    )(need, lows, sinks, mine_q, mine, turned, *caches)
    attn = pl.pallas_call(
        window_kernel,
        out_shape=jax.ShapeDtypeStruct((RING, HD, BLK), jnp.bfloat16),
        in_specs=[smem()] + [vmem()] * 6,
        out_specs=vmem(),
        scratch_shapes=[
            pltpu.VMEM((W, LANES), jnp.bfloat16),
            pltpu.VMEM((W // BLK, HD, BLK), jnp.bfloat16),
        ],
        compiler_params=pltpu.CompilerParams(vmem_limit_bytes=VMEM_LIMIT),
        name="window",
    )(need, lows, mine_q, window, upper, stats, sums)
    attn_t = trade(attn, members).reshape(width, rows)
    give = project(1 - half, attn_t, w_out, jnp.bfloat16)
    got = lax.ppermute(give, "head", [(0, 1), (1, 0)])
    keep = project(half, attn_t, w_out, jnp.float32)
    return (keep + got.astype(jnp.float32)).astype(jnp.bfloat16)


def solution(mesh):
    placed = (
        P("seq", "head"),
        P("seq", "head"),
        P("seq", "head"),
        P("seq", "head"),
        P("seq", "head"),
        P(None, "head"),
        P(None, "head"),
        P(),
        P(),
        P("head", None),
    )
    return jax.shard_map(
        shards, mesh=mesh, in_specs=placed, out_specs=P("head", "seq"), check_vma=False
    )
```

```python
import functools
import math

import jax
import jax.numpy as jnp
from jax import lax
from jax.experimental import pallas as pl
from jax.experimental.pallas import tpu as pltpu
from jax.sharding import PartitionSpec as P

HD = 96
W = 1024
SINKS = 4
G = 2
RING = 16
BLK = 128
QB = 256
CH = 256
LANES = 128
FAR = 1 << 28
LOW = -1e30
VMEM_LIMIT = 24 << 20
PIECE = 256


def pack_kernel(k_ref, v_ref, ck_ref, cv_ref, out_ref):
    heads = k_ref.shape[1] // HD
    for which, ref in enumerate((k_ref, v_ref)):
        turned = ref[...].T
        for p in range(heads):
            out_ref[p, which * HD : (which + 1) * HD, :] = turned[p * HD : (p + 1) * HD, :]
    rows = ck_ref.shape[0]
    fill = jnp.zeros((rows, LANES - HD), ck_ref.dtype)
    for which, ref in enumerate((ck_ref, cv_ref)):
        for p in range(heads):
            piece = jnp.concatenate([ref[:, p * HD : (p + 1) * HD], fill], axis=1)
            base = 2 * HD + which * rows
            out_ref[p, base : base + rows, :] = piece


def gather_facts(place, lengths, groups, need, blocks):
    base = place[0] * RING * BLK
    own = RING * BLK
    for b in range((1 + G) * blocks):
        need[b] = FAR
    need[(1 + G) * blocks] = place[0]

    def one_request(r, carry):
        start, start_col, group_col = carry
        length = lengths[r]
        group = groups[r]
        first = jnp.where(start < base, 0, (start - base) // QB)
        last = jnp.minimum((start + length - 1 - base) // QB, blocks - 1)

        def mark(b, _):
            need[b] = jnp.minimum(need[b], start)
            offset = jnp.maximum(base + b * QB - start, 0)
            at = (1 + group) * blocks + b
            need[at] = jnp.minimum(need[at], offset)
            return 0

        @pl.when((start < base + own) & (start + length > base))
        def _():
            lax.fori_loop(first, last + 1, mark, 0)

        row = lax.broadcasted_iota(jnp.int32, start_col.shape, 0)
        start_col = jnp.where(row == r, start, start_col)
        group_col = jnp.where(row == r, group, group_col)
        return (start + length, start_col, group_col)

    reqs = lengths.shape[0]
    column = jnp.zeros((reqs, QB), jnp.int32)
    _, start_col, group_col = lax.fori_loop(0, reqs, one_request, (jnp.int32(0), column, column))
    return base, start_col, group_col


def query_facts(index, start_col, group_col):
    begun = start_col <= index
    start_q = jnp.max(jnp.where(begun, start_col, 0), axis=0, keepdims=True)
    here = begun & (start_col == start_q)
    group_q = jnp.max(jnp.where(here, group_col, 0), axis=0, keepdims=True)
    return jnp.maximum(start_q, index - (W - 1)), index - start_q, group_q


def turn(piece):
    pad = jnp.zeros((LANES - HD, BLK), jnp.bfloat16)
    return jnp.concatenate([piece, pad], axis=0).T


def query_block(query_ref, b):
    q_t = jnp.concatenate([query_ref[2 * b], query_ref[2 * b + 1]], axis=1)
    return jnp.concatenate([q_t, jnp.zeros((LANES - HD, QB), jnp.bfloat16)], axis=0)


def values(val_ref, at):
    slot = at // BLK
    return jnp.concatenate([val_ref[slot], val_ref[slot + 1]], axis=1)


def dot(a, b):
    return jnp.dot(a, b, preferred_element_type=jnp.float32)


FACTOR = (1.0 / math.sqrt(HD)) * math.log2(math.e)


def prep_kernel(own_ref, key_ref, last_ref):
    for j in range(RING // 2):
        last_ref[j] = own_ref[RING // 2 + j, 0 : 2 * HD, :]
    for j in range(RING):
        key_ref[j * BLK : (j + 1) * BLK, :] = turn(own_ref[j, 0:HD, :])


def pack_query_kernel(
    place, lengths, groups, q_ref, sk_ref, sv_ref, query_ref, sink_ref, low_ref, need
):
    turned = q_ref[...].T
    for p in range(q_ref.shape[1] // HD):
        query_ref[p] = turned[p * HD : (p + 1) * HD, :]
    width = sk_ref.shape[1]
    column = lax.broadcasted_iota(jnp.int32, (width, LANES), 0)
    lane = lax.broadcasted_iota(jnp.int32, (width, LANES), 1)
    pick = ((column == place[1] * HD + lane) & (lane < HD)).astype(jnp.float32).astype(jnp.bfloat16)
    for which, ref in enumerate((sk_ref, sv_ref)):
        piece = jnp.dot(ref[...], pick, preferred_element_type=jnp.float32)
        piece = jnp.concatenate([piece, jnp.zeros_like(piece)], axis=0)
        sink_ref[which * 16 : (which + 1) * 16, :] = piece.astype(jnp.bfloat16)
    own = RING * BLK
    blocks = own // QB
    cache_at = own
    base, start_col, group_col = gather_facts(place, lengths, groups, need, blocks)
    lane = lax.broadcasted_iota(jnp.int32, (1, QB), 1)
    for b in range(blocks):
        index = base + b * QB + lane
        low_q, offset, group_q = query_facts(index, start_col, group_col)
        low_ref[b, 0:1, :] = low_q - base
        for g in range(G):
            low_ref[b, 1 + g : 2 + g, :] = jnp.where(
                group_q == g, cache_at + g * W + offset + 1, FAR
            )
        low_ref[b, 1 + G : 2 + G, :] = jnp.full((1, QB), FAR, jnp.int32)
        low_ref[b, 2 + G : 3 + G, :] = group_q


def fold(rows, how):
    return how(rows.reshape(rows.shape[0] // 8, 8, QB), axis=0)


def visit(total, where_is, key_ref, val_ref, low_of, q_t, state, buffers):
    s_even, s_odd, p_even, p_odd = buffers
    row_iota = lax.broadcasted_iota(jnp.int32, (PIECE, QB), 0)
    pieces = [slice(n * PIECE, (n + 1) * PIECE) for n in range(CH // PIECE)]

    def scores(j, ref):
        at, kind = where_is(j)
        low = low_of(kind) - at
        peak = None
        for n, rows in enumerate(pieces):
            s = dot(key_ref[pl.ds(at + n * PIECE, PIECE), :], q_t)
            s = jnp.where(row_iota >= low - n * PIECE, s, LOW)
            ref[rows, :] = s
            high = fold(s, jnp.max)
            peak = high if peak is None else jnp.maximum(peak, high)
        return peak, at

    def weigh(s_ref, p_ref, peak, top, den):
        new = jnp.maximum(top, jnp.max(peak, axis=0, keepdims=True))
        fade = jnp.exp2((top - new) * FACTOR)
        den = den * fade
        for rows in pieces:
            p = jnp.exp2((s_ref[rows, :] - new) * FACTOR)
            den = den + fold(p, jnp.sum)
            p_ref[rows, :] = p.astype(jnp.bfloat16)
        return new, fade, den

    top, den, acc, before = state
    peak, at = scores(0, s_even)

    def step(j, state):
        top, den, acc, before, peak, at = state
        next_peak, next_at = scores(2 * j + 1, s_odd)
        acc = acc + dot(values(val_ref, before), p_odd[...])
        top, fade, den = weigh(s_even, p_even, peak, top, den)
        acc = acc * fade + dot(values(val_ref, at), p_even[...])
        peak, last_at = scores(2 * j + 2, s_even)
        top, fade, den = weigh(s_odd, p_odd, next_peak, top, den)
        acc = acc * fade
        return (top, den, acc, next_at, peak, last_at)

    top, den, acc, before, _, _ = lax.fori_loop(
        0, (total + 1) // 2, step, (top, den, acc, before, peak, at)
    )
    return top, den, acc + dot(values(val_ref, before), p_odd[...])


def visit_plain(total, where_is, key_ref, val_ref, low_of, q_t, state):
    row_iota = lax.broadcasted_iota(jnp.int32, (CH, QB), 0)

    def step(j, state):
        top, den, acc = state
        scores, ats = [], []
        for u in range(2):
            at, kind = where_is(2 * j + u)
            s = dot(key_ref[pl.ds(at, CH), :], q_t)
            scores.append(jnp.where(row_iota >= low_of(kind) - at, s, LOW))
            ats.append(at)
        peak = jnp.maximum(fold(scores[0], jnp.max), fold(scores[1], jnp.max))
        new = jnp.maximum(top, jnp.max(peak, axis=0, keepdims=True))
        fade = jnp.exp2((top - new) * FACTOR)
        den = den * fade
        ps = []
        for u in range(2):
            p = jnp.exp2((scores[u] - new) * FACTOR)
            den = den + fold(p, jnp.sum)
            ps.append(p.astype(jnp.bfloat16))
        vals = jnp.concatenate([values(val_ref, at) for at in ats], axis=1)
        acc = acc * fade + dot(vals, jnp.concatenate(ps, axis=0))
        return (new, den, acc)

    return lax.fori_loop(0, (total + 1) // 2, step, state)


def attend_kernel(
    need, low_ref, sink_ref, query_ref, own_ref, turned_ref, *rest, rings
):
    caches = rest[:rings]
    upper_ref, stat_ref, acc_ref, key_ref, val_ref = rest[rings : rings + 5]
    buffers = rest[rings + 5 :]
    own = RING * BLK
    blocks = own // QB
    ring = need[(1 + G) * blocks]
    base = ring * own
    key_ref[0:own, :] = turned_ref[...]
    for j in range(RING):
        val_ref[j] = own_ref[j, HD : 2 * HD, :]
    rows = RING * 16
    for k in range(rings):
        source = lax.rem(lax.rem(ring, 4) + k % 4, 4) + 4 * lax.rem(ring // 4 + k // 4, 2)
        piece = caches[k][...]
        at = pl.multiple_of(own + source * rows, rows)
        key_ref[pl.ds(at, rows), :] = piece[:, 0:16, :].reshape(rows, LANES)
        turned = piece[:, 16:32, :].reshape(rows, LANES).T
        for half in range(rows // BLK):
            val_ref[at // BLK + half] = turned[0:HD, half * BLK : (half + 1) * BLK]
    lane = lax.broadcasted_iota(jnp.int32, (1, QB), 1)
    row_iota = lax.broadcasted_iota(jnp.int32, (CH, QB), 0)
    sink_row = lax.broadcasted_iota(jnp.int32, (16, QB), 0)
    sink_v = sink_ref[16:32, :].T[0:HD, :]

    def one_block(b):
        low_suffix = low_ref[b, 0:1, :]
        group_q = low_ref[b, 2 + G : 3 + G, :]
        q_t = query_block(query_ref, b)
        at0 = pl.multiple_of(b * QB, CH)
        s_d = dot(key_ref[pl.ds(at0, CH), :], q_t)
        s_d = jnp.where((row_iota >= low_suffix - at0) & (row_iota <= lane), s_d, LOW)
        s_s = dot(sink_ref[0:16, :], q_t)
        s_s = jnp.where((sink_row // SINKS == group_q) & (sink_row < G * SINKS), s_s, LOW)
        top = jnp.maximum(jnp.max(s_d, axis=0, keepdims=True), jnp.max(s_s, axis=0, keepdims=True))
        p_d = jnp.exp2((s_d - top) * FACTOR)
        p_s = jnp.exp2((s_s - top) * FACTOR)
        den = fold(p_d, jnp.sum) + fold(p_s, jnp.sum)
        buffers[3][...] = p_d.astype(jnp.bfloat16)
        acc = dot(sink_v, p_s.astype(jnp.bfloat16))

        first = jnp.maximum(jnp.maximum(need[b] - base, b * QB - (W - 1)), 0) // CH
        n_suffix = b - first
        c0 = [jnp.minimum((need[(1 + g) * blocks + b] + 1) // CH, W // CH) for g in range(G)]
        n0, n1 = [W // CH - c for c in c0]
        total = n_suffix + n0 + n1

        def where_is(j):
            in0 = j - n_suffix
            in1 = in0 - n0
            at = jnp.where(
                in0 < 0,
                (first + j) * CH,
                jnp.where(
                    in1 < 0,
                    own + (c0[0] + in0) * CH,
                    jnp.where(j < total, own + W + (c0[1] + in1) * CH, 0),
                ),
            )
            kind = jnp.where(in0 < 0, 0, jnp.where(in1 < 0, 1, jnp.where(j < total, 2, 3)))
            return pl.multiple_of(at, CH), kind

        def low_of(kind):
            return low_ref[b, pl.ds(kind, 1), :]

        state = (top, den, acc, at0)
        top, den, acc = visit(total, where_is, key_ref, val_ref, low_of, q_t, state, buffers)

        @pl.when(b < blocks // 2)
        def _():
            stat_ref[b, 0:8, :] = jnp.broadcast_to(top, (8, QB))
            stat_ref[b, 8:16, :] = den
            acc_ref[b] = acc

        @pl.when(b >= blocks // 2)
        def _():
            done = (acc / jnp.sum(den, axis=0, keepdims=True)).astype(jnp.bfloat16)
            upper_ref[2 * b - RING // 2] = done[:, 0:BLK]
            upper_ref[2 * b + 1 - RING // 2] = done[:, BLK:QB]

        return 0

    for b in range(blocks):
        one_block(b)


def window_kernel(
    need, low_ref, query_ref, win_ref, upper_ref, stat_ref, acc_ref, out_ref,
    key_ref, val_ref,
):
    blocks = RING * BLK // QB
    base = need[(1 + G) * blocks] * RING * BLK
    for j in range(RING // 2):
        key_ref[j * BLK : (j + 1) * BLK, :] = turn(win_ref[j, 0:HD, :])
        val_ref[j] = win_ref[j, HD : 2 * HD, :]
        out_ref[RING // 2 + j] = upper_ref[j]

    def one_block(b):
        q_t = query_block(query_ref, b)
        first = jnp.maximum(need[b] - base, b * QB - (W - 1)) + W
        first = jnp.minimum(first // CH, W // CH)
        total = W // CH - first

        def where_is(j):
            at = jnp.where(j < total, (first + j) * CH, 0)
            return pl.multiple_of(at, CH), jnp.where(j < total, 0, 1 + G)

        def low_of(kind):
            return low_ref[b, pl.ds(kind, 1), :] + jnp.where(kind == 0, W, 0)

        state = (stat_ref[b, 0:1, :], stat_ref[b, 8:16, :], acc_ref[b])
        _, den, acc = visit_plain(total, where_is, key_ref, val_ref, low_of, q_t, state)
        done = (acc / jnp.sum(den, axis=0, keepdims=True)).astype(jnp.bfloat16)
        out_ref[2 * b] = done[:, 0:BLK]
        out_ref[2 * b + 1] = done[:, BLK:QB]
        return 0

    for b in range(blocks // 2):
        one_block(b)


def project_kernel(side, attn_ref, w_ref, out_ref, half_ref, sum_ref, arrived):
    features = half_ref.shape[1]
    columns = pl.ds(pl.multiple_of(side[0] * features, features), features)
    parts = arrived.shape[0]
    tall = half_ref.shape[0] // parts
    loads = []
    for n in range(parts):
        rows = pl.ds(n * tall, tall)
        loads.append(
            pltpu.make_async_copy(w_ref.at[rows, columns], half_ref.at[rows, :], arrived.at[n])
        )
    for load in loads:
        load.start()
    turned = attn_ref[...].T
    for n in range(parts):
        loads[n].wait()
        at = slice(n * tall, (n + 1) * tall)
        part = dot(turned[:, at], half_ref[at, :])
        if n == 0:
            sum_ref[...] = part
        elif n < parts - 1:
            sum_ref[...] += part
        else:
            out_ref[...] = (sum_ref[...] + part).T.astype(out_ref.dtype)


def project(side, attn_t, w_out, dtype, features):
    width, rows = attn_t.shape
    return pl.pallas_call(
        project_kernel,
        out_shape=jax.ShapeDtypeStruct((features, rows), dtype),
        in_specs=[smem(), vmem(), pl.BlockSpec(memory_space=pltpu.HBM)],
        out_specs=vmem(),
        scratch_shapes=[
            pltpu.VMEM((width, features), jnp.bfloat16),
            pltpu.VMEM((rows, features), jnp.float32),
            pltpu.SemaphoreType.DMA((6,)),
        ],
        cost_estimate=pl.CostEstimate(
            flops=2 * width * features * rows,
            bytes_accessed=2 * width * features,
            transcendentals=0,
        ),
        compiler_params=pltpu.CompilerParams(vmem_limit_bytes=50 << 20),
        name="project",
    )(side.reshape(1), attn_t, w_out)


def vmem():
    return pl.BlockSpec(memory_space=pltpu.VMEM)


def smem():
    return pl.BlockSpec(memory_space=pltpu.SMEM)


def shards(
    queries, keys, values, cache_k, cache_v, sink_k, sink_v, suffix_lengths, request_group, w_out
):
    rows, width = queries.shape
    heads = width // HD
    seq = lax.axis_size("seq")
    rings = seq // RING
    device = lax.axis_index("seq")
    half = lax.axis_index("head")
    packed = pl.pallas_call(
        pack_kernel,
        out_shape=jax.ShapeDtypeStruct((heads, 2 * HD + 32, LANES), jnp.bfloat16),
        in_specs=[vmem()] * 4,
        out_specs=vmem(),
        name="pack",
    )(keys, values, cache_k, cache_v)
    own = RING * BLK
    blocks = own // QB
    place = jnp.stack([device // RING, device % RING]).astype(jnp.int32)
    packed_q, sinks, lows, need = pl.pallas_call(
        pack_query_kernel,
        out_shape=(
            jax.ShapeDtypeStruct((heads, HD, LANES), jnp.bfloat16),
            jax.ShapeDtypeStruct((32, LANES), jnp.bfloat16),
            jax.ShapeDtypeStruct((blocks, 8, QB), jnp.int32),
            jax.ShapeDtypeStruct(((1 + G) * blocks + 1,), jnp.int32),
        ),
        in_specs=[smem()] * 3 + [vmem()] * 3,
        out_specs=(vmem(), vmem(), vmem(), smem()),
        cost_estimate=pl.CostEstimate(flops=1 << 20, bytes_accessed=1 << 21, transcendentals=0),
        compiler_params=pltpu.CompilerParams(vmem_limit_bytes=VMEM_LIMIT),
        name="pack_query",
    )(place, suffix_lengths, request_group, queries, sink_k, sink_v)
    members = [[r * RING + i for i in range(RING)] for r in range(rings)]

    def trade(array, groups):
        return lax.all_to_all(array, "seq", 0, 0, axis_index_groups=groups, tiled=True)

    mine = trade(packed, members)
    mine_q = trade(packed_q, members)
    cache = mine[:, 2 * HD :, :]

    def send(array, dx, dy):
        pairs = []
        for r in range(rings):
            to = (r % 4 + dy) % 4 + 4 * ((r // 4 + dx) % 2)
            pairs += [(r * RING + i, to * RING + i) for i in range(RING)]
        return lax.ppermute(array, "seq", pairs)

    near_y = send(cache, 0, 3)
    near_x = send(cache, 1, 0)
    back_y = send(cache, 0, 1)
    far_y = send(cache, 0, 2)
    near_xy = send(near_x, 0, 3)
    back_xy = send(back_y, 1, 0)
    far_xy = send(far_y, 1, 0)
    caches = [cache, near_y, far_y, back_y, near_x, near_xy, far_xy, back_xy]
    turned, last = pl.pallas_call(
        prep_kernel,
        out_shape=(
            jax.ShapeDtypeStruct((own, LANES), jnp.bfloat16),
            jax.ShapeDtypeStruct((RING // 2, 2 * HD, LANES), jnp.bfloat16),
        ),
        in_specs=[vmem()],
        out_specs=(vmem(), vmem()),
        cost_estimate=pl.CostEstimate(
            flops=1 << 20, bytes_accessed=1 << 22, transcendentals=0
        ),
        compiler_params=pltpu.CompilerParams(vmem_limit_bytes=VMEM_LIMIT),
        name="prep",
    )(mine)
    window = lax.ppermute(last, "seq", [(s, s + RING) for s in range(seq - RING)])
    buffers = [pltpu.VMEM((CH, QB), jnp.float32)] * 2 + [pltpu.VMEM((CH, QB), jnp.bfloat16)] * 2
    upper, stats, sums = pl.pallas_call(
        functools.partial(attend_kernel, rings=rings),
        out_shape=(
            jax.ShapeDtypeStruct((RING // 2, HD, BLK), jnp.bfloat16),
            jax.ShapeDtypeStruct((blocks // 2, 16, QB), jnp.float32),
            jax.ShapeDtypeStruct((blocks // 2, HD, QB), jnp.float32),
        ),
        in_specs=[smem()] + [vmem()] * (5 + rings),
        out_specs=(vmem(), vmem(), vmem()),
        scratch_shapes=[
            pltpu.VMEM((own + G * W, LANES), jnp.bfloat16),
            pltpu.VMEM(((own + G * W) // BLK, HD, BLK), jnp.bfloat16),
            *buffers,
        ],
        cost_estimate=pl.CostEstimate(
            flops=own * 2 * W * HD * 4, bytes_accessed=1 << 22, transcendentals=own * 2 * W
        ),
        compiler_params=pltpu.CompilerParams(vmem_limit_bytes=VMEM_LIMIT),
        name="attend",
    )(need, lows, sinks, mine_q, mine, turned, *caches)
    attn = pl.pallas_call(
        window_kernel,
        out_shape=jax.ShapeDtypeStruct((RING, HD, BLK), jnp.bfloat16),
        in_specs=[smem()] + [vmem()] * 6,
        out_specs=vmem(),
        scratch_shapes=[
            pltpu.VMEM((W, LANES), jnp.bfloat16),
            pltpu.VMEM((W // BLK, HD, BLK), jnp.bfloat16),
        ],
        compiler_params=pltpu.CompilerParams(vmem_limit_bytes=VMEM_LIMIT),
        name="window",
    )(need, lows, mine_q, window, upper, stats, sums)
    attn_t = trade(attn, members).reshape(width, rows)
    features = w_out.shape[1] // 2
    got = []
    for n in range(2):
        give = project(2 * (1 - half) + n, attn_t, w_out, jnp.bfloat16, features // 2)
        got.append(lax.ppermute(give, "head", [(0, 1), (1, 0)]))
    got = jnp.concatenate(got, axis=0)
    keep = project(half, attn_t, w_out, jnp.float32, features)
    return (keep + got.astype(jnp.float32)).astype(jnp.bfloat16)


def solution(mesh):
    placed = (
        P("seq", "head"),
        P("seq", "head"),
        P("seq", "head"),
        P("seq", "head"),
        P("seq", "head"),
        P(None, "head"),
        P(None, "head"),
        P(),
        P(),
        P("head", None),
    )
    return jax.shard_map(
        shards, mesh=mesh, in_specs=placed, out_specs=P("head", "seq"), check_vma=False
    )
```
